128 devices in a mesh: drift: 8 (over x, core), beam: 16 (over z, y).
Axes of the slice: x: 4, y: 4, z: 4, core: 2. Of those that a mesh axis runs over, the one named last changes fastest.
Arguments:
- features: bfloat16 [64, 32, 256, 128], P('drift', None, 'beam'), may hold values from -6 to 6
- occupied: int32 [8, 32, 16], P('drift', 'beam'), may hold values 0 or 1
- voxel_fragment: int32 [64, 256, 128], P('drift', 'beam'), may hold values from 0 to 4095, as said below
- conv_weight: bfloat16 [32, 864], replicated, may hold values from -0.21875 to 0.21875
- embed_weight: bfloat16 [32, 256], replicated, may hold values from -6 to 6
- message_weight: bfloat16 [256, 256], replicated, may hold values from -0.375 to 0.375
- update_weight: bfloat16 [256, 256], replicated, may hold values from -0.375 to 0.375
- edge_source: int32 [131072], P(('drift', 'beam')), may hold values from 0 to 4095
- edge_target: int32 [131072], P(('drift', 'beam')), may hold values from 0 to 255
- out_cotangent: bfloat16 [32768, 256], P(('drift', 'beam')), may hold values from -6 to 6
Outputs:
- fragment_out: bfloat16 [32768, 256], P(('drift', 'beam'))
- grad_features: float32 [64, 32, 256, 128], P('drift', None, 'beam')
- grad_conv: float32 [32, 864], replicated
The draws below stay inside these ranges and needn't reach their ends.
Inputs may be any that keep to these rules, and one draw needn't show every extreme that they name: `voxel_fragment`: index among the 4096 fragments of the voxel's drift row.
All inputs are finite; a program needn't handle non-finite values. No bound on the sum of `occupied` on one device may be relied on, other than what follows from the above.
Results may differ from the reference program's by a relative error of at most 0.01.
Values may be sent and summed in bfloat16 or wider, within the bound.
A program may use at most 64 MiB of HBM per device.

```python
import jax
import jax.numpy as jnp
from jax import lax

C = 32
HID = 256
BLOCK = 8
TX = 8
TY = 16
FRAG_DEV = 256
EDGE_DEV = 1024
NX = 64
NY = 256
NZ = 128
FRAG_ROW = 4096
FRAGS = 32768
EDGES = 131072
N_BEAM = 16


def draw_voxel_fragment(key, part):
    tiles = NY // TY
    shape = (NX, NY, NZ)
    column = (jnp.arange(NY, dtype=jnp.int32) // TY)[None, :, None]
    near = jax.random.randint(jax.random.fold_in(key, 11), shape, -1, 2)
    far = jax.random.randint(jax.random.fold_in(key, 12), shape, 0, tiles)
    pick = jax.random.randint(jax.random.fold_in(key, 13), shape, 0, 10)
    owner = jnp.where(pick < 7, (column + near + tiles) % tiles, far)
    first = jax.random.randint(jax.random.fold_in(key, 14), shape, 0, FRAG_DEV)
    second = jax.random.randint(jax.random.fold_in(key, 15), shape, 0, FRAG_DEV)
    local = first * second // FRAG_DEV
    return (owner * FRAG_DEV + local).astype(jnp.int32)


def with_ends(values, rng, least, largest):
    longest = values.shape.index(max(values.shape))
    spots = []
    for shift in (0, 1):
        where = [jax.random.randint(jax.random.fold_in(rng, axis), (), 0, length) for axis, length in enumerate(values.shape)]
        where[longest] = (where[longest] + shift) % values.shape[longest]
        spots.append(tuple(where))
    return values.at[spots[0]].set(least).at[spots[1]].set(largest)


def steps_of(key, extent, shards, least, high):
    gain = 1.0
    for position, blocks in shards:
        draws = jax.random.uniform(jax.random.fold_in(jax.random.fold_in(key, 6), position), (blocks,), jnp.float32, least / len(shards), high / len(shards))
        gain = gain * jnp.repeat(jnp.exp(draws), extent[position] // blocks).reshape((-1,) + (1,) * (len(extent) - 1 - position))
    return gain


def normal_values(key, dims, deviation, limit, shards=(), held_as=jnp.bfloat16):
    drawn = jax.random.normal(key, dims, jnp.float32) * deviation
    if len(shards) > 0:
        drawn = steps_of(key, dims, shards, -0.22, 0.18) * drawn
    return jnp.clip(drawn, min=-limit, max=limit).astype(held_as)


def setup_inputs(seed: int = 0) -> dict:
    streams_of = jax.random.split(jax.random.key(seed), 11)
    return {
        "features": normal_values(streams_of[0], (NX, C, NY, NZ), 1.0, 6.0, ((0, 8), (2, 16))),
        "occupied": with_ends((jax.random.randint(streams_of[1], (NX // BLOCK, NY // BLOCK, NZ // BLOCK), 0, 8) < 5).astype(jnp.int32), jax.random.fold_in(streams_of[1], 1), 0, 1),
        "voxel_fragment": draw_voxel_fragment(jax.random.fold_in(streams_of[10], 71), 0),
        "conv_weight": normal_values(streams_of[3], (C, 27 * C), (27 * C) ** -0.5, 0.21875),
        "embed_weight": normal_values(streams_of[4], (C, HID), 1 ** -0.5, 6.0),
        "message_weight": normal_values(streams_of[5], (HID, HID), HID ** -0.5, 0.375),
        "update_weight": normal_values(streams_of[6], (HID, HID), HID ** -0.5, 0.375),
        "edge_source": with_ends(jax.random.randint(streams_of[7], (EDGES,), 0, FRAG_ROW), jax.random.fold_in(streams_of[7], 1), 0, FRAG_ROW - 1).astype(jnp.int32),
        "edge_target": with_ends(jax.random.randint(streams_of[8], (EDGES,), 0, FRAG_DEV), jax.random.fold_in(streams_of[8], 1), 0, FRAG_DEV - 1).astype(jnp.int32),
        "out_cotangent": normal_values(streams_of[9], (FRAGS, HID), 1.0, 6.0, ((0, 128),)),
    }


def slope(value):
    sig = jax.nn.sigmoid(value)
    return sig * (1.0 + value * (1.0 - sig))


def columns(padded, row):
    channels = padded.shape[1]
    height = padded.shape[2] - 2
    depth = padded.shape[3] - 2
    anchor = jnp.zeros((), jnp.int32)
    start_row = anchor + row
    pieces = []
    for off_a in range(3):
        for off_b in range(3):
            for off_c in range(3):
                index = (start_row + off_a, anchor, anchor + off_b, anchor + off_c)
                piece = lax.dynamic_slice(padded, index, (1, channels, height, depth))
                pieces.append(piece.reshape(channels, height * depth))
    return jnp.concatenate(pieces, 0)


def convolve(padded, weight):
    rows = padded.shape[0] - 2
    height = padded.shape[2] - 2
    depth = padded.shape[3] - 2
    wide = weight.astype(jnp.float32)

    def one_row(row):
        cols = columns(padded, row).astype(jnp.float32)
        return jnp.dot(wide, cols, precision=lax.Precision.HIGHEST)

    result = lax.map(one_row, jnp.arange(rows, dtype=jnp.int32))
    return result.reshape(rows, weight.shape[0], height, depth)


def reference(features, occupied, voxel_fragment, conv_weight, embed_weight, message_weight, update_weight, edge_source, edge_target, out_cotangent):
    f32 = jnp.float32
    mask = jnp.repeat(jnp.repeat(jnp.repeat(occupied, BLOCK, 0), BLOCK, 1), BLOCK, 2).astype(f32)
    mask_four = mask[:, None]
    active = features * mask_four.astype(features.dtype)
    padded = jnp.pad(active, ((1, 1), (0, 0), (1, 1), (1, 1)))
    conv_out = convolve(padded, conv_weight)
    hidden = mask_four * (active.astype(f32) + jax.nn.silu(conv_out))
    row_of = jnp.arange(NX, dtype=jnp.int32) // TX
    frag_ids = (row_of[:, None, None] * FRAG_ROW + voxel_fragment).reshape(-1).astype(jnp.int32)
    by_voxel = hidden.transpose(0, 2, 3, 1).reshape(-1, C)
    sums = jax.ops.segment_sum(by_voxel, frag_ids, num_segments=FRAGS)
    counts = jax.ops.segment_sum(mask.reshape(-1), frag_ids, num_segments=FRAGS)
    divisor = jnp.maximum(counts, 1.0)[:, None]
    pooled = (sums / divisor).astype(jnp.bfloat16)
    pre_own = jnp.dot(pooled, embed_weight, preferred_element_type=f32)
    own = jax.nn.silu(pre_own).astype(jnp.bfloat16)
    device = jnp.arange(EDGES, dtype=jnp.int32) // EDGE_DEV
    drift_row = device // N_BEAM
    beam_col = device % N_BEAM
    src = (drift_row * FRAG_ROW + edge_source).astype(jnp.int32)
    dst = (drift_row * FRAG_ROW + beam_col * FRAG_DEV + edge_target).astype(jnp.int32)
    pre_msg = jnp.dot(own[src], message_weight, preferred_element_type=f32)
    messages = jax.nn.silu(pre_msg).astype(jnp.bfloat16)
    gathered = jax.ops.segment_sum(messages.astype(f32), dst, num_segments=FRAGS).astype(jnp.bfloat16)
    fragment_out = (own.astype(f32) + jnp.dot(gathered, update_weight, preferred_element_type=f32)).astype(jnp.bfloat16)
    back_agg = jnp.dot(out_cotangent, update_weight.T, preferred_element_type=f32).astype(jnp.bfloat16)
    back_pre = (back_agg[dst].astype(f32) * slope(pre_msg)).astype(jnp.bfloat16)
    back_src = jnp.dot(back_pre, message_weight.T, preferred_element_type=f32)
    back_own = out_cotangent.astype(f32) + jax.ops.segment_sum(back_src, src, num_segments=FRAGS)
    back_pooled = jnp.dot(back_own * slope(pre_own), embed_weight.astype(f32).T, precision=lax.Precision.HIGHEST)
    back_mean = back_pooled / divisor
    back_hidden = back_mean[frag_ids].reshape(NX, NY, NZ, C).transpose(0, 3, 1, 2)
    back_conv = (mask_four * back_hidden * slope(conv_out)).astype(jnp.bfloat16)
    padded_grad = jnp.pad(back_conv, ((1, 1), (0, 0), (1, 1), (1, 1)))
    flipped = conv_weight.reshape(C, 27, C)[:, ::-1, :].transpose(2, 1, 0).reshape(C, 27 * C)
    back_active = mask_four * back_hidden + convolve(padded_grad, flipped)
    grad_features = mask_four * back_active

    def accumulate(total, row):
        cols = columns(padded, row).astype(f32)
        slab = lax.dynamic_index_in_dim(back_conv, row, 0, keepdims=False).reshape(C, -1).astype(f32)
        term = lax.dot_general(slab, cols, (((1,), (1,)), ((), ())), precision=lax.Precision.HIGHEST)
        return total + term, None

    grad_conv, _ = lax.scan(accumulate, jnp.zeros((C, 27 * C), f32), jnp.arange(NX, dtype=jnp.int32))
    return fragment_out, grad_features, grad_conv
```

```python
import functools

import jax
import jax.numpy as jnp
from jax import lax
from jax.experimental import pallas as pl
from jax.experimental.pallas import tpu as pltpu
from jax.sharding import PartitionSpec as P

F32 = jnp.float32
BF16 = jnp.bfloat16
MESH = pl.DeviceIdType.MESH
C = 32
YB = 4
WIN = (YB + 2) * 3 * C
KC = 3 * WIN
NN = (((1,), (0,)), ((), ()))
NT = (((1,), (1,)), ((), ()))
TN = (((0,), (0,)), ((), ()))


def mm(lhs, rhs, dims):
    return lax.dot_general(lhs, rhs, dims, preferred_element_type=F32)


def sig_parts(value):
    sig = 1.0 / (1.0 + jnp.exp(-value))
    return value * sig, sig * (1.0 + value * (1.0 - sig))


def spread(cols, x, row, tile, lane):
    left = jnp.where(lane == 0, 0.0, pltpu.roll(tile, 1, 1)).astype(BF16)
    right = jnp.where(lane == 127, 0.0, pltpu.roll(tile, 127, 1)).astype(BF16)
    mid = tile.astype(BF16)
    for half in range(2):
        for k in range(2):
            inner = row - 8 * half - 4 * k
            if 0 <= inner < YB + 2:
                for tap, part in enumerate((left, mid, right)):
                    start = pl.multiple_of(x * WIN + inner * 96 + tap * C, C)
                    cols[k, pl.ds(start, C), half * 128 : half * 128 + 128] = part


def widen(wide, weight):
    wide[...] = jnp.zeros_like(wide)
    for yo in range(YB):
        for a in range(3):
            at = a * WIN + yo * 96
            wide[yo * C : yo * C + C, at : at + 288] = weight[:, a * 288 : a * 288 + 288]


def kernel(
    nd,
    nb,
    feat,
    occ,
    vf,
    cw,
    cwf,
    emb,
    mw,
    uw,
    es,
    et,
    cot,
    fo,
    gf,
    gc,
    stage,
    plain,
    cols,
    gcols,
    wide,
    gwide,
    lohot,
    ahot,
    slopes,
    bh,
    bc,
    res,
    sums,
    gbig,
    hx,
    hy,
    hc,
    gx,
    gy,
    gcn,
    cs,
    cr,
    ms,
    mr,
    pa,
    ms2,
    mr2,
    bm,
    gs,
    g1,
    g2s,
    g2,
    g3,
    hs,
    hr,
    ks,
    kr,
    ps,
    pr,
):
    d = lax.axis_index("drift")
    b = lax.axis_index("beam")
    dn, dp = lax.rem(d + 1, nd), lax.rem(d + nd - 1, nd)
    bn, bp = lax.rem(b + 1, nb), lax.rem(b + nb - 1, nb)

    barrier = pltpu.get_barrier_semaphore()

    def greet(dev):
        pl.semaphore_signal(barrier, inc=1, device_id=dev, device_id_type=MESH)

    def greet_beam(off, carry):
        greet((d, lax.rem(b + off, nb)))
        return carry

    def greet_drift(off, carry):
        greet((lax.rem(d + off, nd), b))
        return carry

    lax.fori_loop(1, nb, greet_beam, 0)
    lax.fori_loop(1, nd, greet_drift, 0)
    for dev in ((dn, bn), (dn, bp), (dp, bn), (dp, bp)):
        greet(dev)
    pl.semaphore_wait(barrier, nb - 1 + nd - 1 + 4)

    lane = lax.broadcasted_iota(jnp.int32, (C, 128), 1)
    group = lax.broadcasted_iota(jnp.int32, (1, 128), 1) // 8
    occ_f = occ[...].astype(F32)
    rows = []
    for j in range(2):
        row = jnp.zeros((1, 128), F32)
        for q in range(16):
            row = jnp.where(group == q, occ_f[j : j + 1, q : q + 1], row)
        rows.append(row)
    mrow = jnp.concatenate(rows, axis=1)
    x_lo = jnp.where(d > 0, 1.0, 0.0).astype(F32)
    x_hi = jnp.where(d < nd - 1, 1.0, 0.0).astype(F32)
    y_lo = jnp.where(b > 0, 1.0, 0.0).astype(F32)
    y_hi = jnp.where(b < nb - 1, 1.0, 0.0).astype(F32)

    def halo_copies(src, tx, ty, tc, base):
        plan = (
            (src.at[7], tx.at[0], (dn, b)),
            (src.at[0], tx.at[1], (dp, b)),
            (src.at[:, 480:512, :], ty.at[0], (d, bn)),
            (src.at[:, 0:32, :], ty.at[1], (d, bp)),
            (src.at[7, 480:512, :], tc.at[0], (dn, bn)),
            (src.at[7, 0:32, :], tc.at[1], (dn, bp)),
            (src.at[0, 480:512, :], tc.at[2], (dp, bn)),
            (src.at[0, 0:32, :], tc.at[3], (dp, bp)),
        )
        return [
            pltpu.make_async_remote_copy(
                src_ref=s,
                dst_ref=t,
                send_sem=hs.at[base + i],
                recv_sem=hr.at[base + i],
                device_id=dev,
                device_id_type=MESH,
            )
            for i, (s, t, dev) in enumerate(plan)
        ]

    def place_halos(target, tx, ty, tc):
        for y in range(16):
            spread(target, 0, y + 1, tx[0, y * C : y * C + C, :].astype(F32) * x_lo, lane)
            spread(target, 9, y + 1, tx[1, y * C : y * C + C, :].astype(F32) * x_hi, lane)

        def per_x(x, carry):
            spread(target, x + 1, 0, ty[0, x].astype(F32) * y_lo, lane)
            spread(target, x + 1, 17, ty[1, x].astype(F32) * y_hi, lane)
            return carry

        lax.fori_loop(0, 8, per_x, 0)
        spread(target, 0, 0, tc[0].astype(F32) * (x_lo * y_lo), lane)
        spread(target, 0, 17, tc[1].astype(F32) * (x_lo * y_hi), lane)
        spread(target, 9, 0, tc[2].astype(F32) * (x_hi * y_lo), lane)
        spread(target, 9, 17, tc[3].astype(F32) * (x_hi * y_hi), lane)

    def beam_copy(src, dst, base):
        def make(off):
            peer = lax.rem(b + off, nb)
            return pltpu.make_async_remote_copy(
                src_ref=src(peer),
                dst_ref=dst,
                send_sem=ks.at[base, off],
                recv_sem=kr.at[base, off],
                device_id=(d, peer),
                device_id_type=MESH,
            )

        return make

    def drift_copy(src, dst):
        def make(off):
            peer = lax.rem(d + off, nd)
            return pltpu.make_async_remote_copy(
                src_ref=src,
                dst_ref=dst,
                send_sem=ps.at[off],
                recv_sem=pr.at[off],
                device_id=(peer, b),
                device_id_type=MESH,
            )

        return make

    def start_all(make, count):
        def step(off, carry):
            make(off).start()
            return carry

        lax.fori_loop(1, count, step, 0)

    def wait_all(make, count):
        def step(off, carry):
            make(off).wait()
            return carry

        lax.fori_loop(1, count, step, 0)

    def load_row(x, carry):
        stage[...] = feat[x].astype(F32)
        for y in range(16):
            h = y // 8
            tile = stage[pl.ds(y, C, stride=16), :] * mrow[:, h * 128 : h * 128 + 128]
            plain[0, x, y * C : y * C + C, :] = tile.astype(BF16)
            spread(cols, x + 1, y + 1, tile, lane)
        return carry

    lax.fori_loop(0, 8, load_row, 0)
    halos = halo_copies(plain.at[0], hx, hy, hc, 0)
    for copy in halos:
        copy.start()

    sub_lo = lax.broadcasted_iota(jnp.int32, (256, 256), 0)
    sub_hi = lax.broadcasted_iota(jnp.int32, (16, 256), 0)

    def fids(x):
        return jnp.concatenate([vf[x, 0:8, :], vf[x, 8:16, :]], axis=1)

    def counts_of(x, total):
        ids = fids(x)
        for k in range(2):
            parts = []
            for yo in range(YB):
                r = k * YB + yo
                one = ids[r : r + 1, :]
                lo = one & 255
                hi = one >> 8
                lohot[2 * x + k, :, yo * 256 : yo * 256 + 256] = (sub_lo == lo).astype(F32).astype(BF16)
                parts.append(jnp.where(sub_hi == hi, mrow, 0.0).astype(BF16))
            total = total + mm(jnp.concatenate(parts, axis=1), lohot[2 * x + k], NT)
        return total

    counts = lax.fori_loop(0, 8, counts_of, jnp.zeros((16, 256), F32))
    for j in range(16):
        cs[j] = jnp.broadcast_to(counts[j : j + 1, :], (8, 256))
    cr[b] = cs[b]
    count_copies = beam_copy(lambda peer: cs.at[peer], cr.at[b], 0)
    start_all(count_copies, nb)

    widen(wide, cw)
    widen(gwide, cwf)
    for copy in halos:
        copy.wait()
    place_halos(cols, hx, hy, hc)

    sums[...] = jnp.zeros_like(sums)

    def forward(x, carry):
        ids = fids(x)
        for k in range(2):
            g = 2 * x + k
            start = pl.multiple_of(x * WIN, C)
            conv = mm(wide[...], cols[k, pl.ds(start, KC), :], NN)
            silu, slope = sig_parts(conv)
            slopes[g] = slope * mrow
            for yo in range(YB):
                at = pl.multiple_of((x + 1) * WIN + (yo + 1) * 96 + C, C)
                act = cols[k, pl.ds(at, C), :].astype(F32)
                hid = mrow * (act + silu[yo * C : yo * C + C, :])
                r = k * YB + yo
                hi = ids[r : r + 1, :] >> 8
                for q in range(16):
                    ahot[q * C : q * C + C, yo * 256 : yo * 256 + 256] = jnp.where(
                        hi == q, hid, 0.0
                    ).astype(BF16)
            sums[...] += mm(ahot[...], lohot[g], NT)
        return carry

    lax.fori_loop(0, 8, forward, 0)
    for j in range(16):
        ms[j] = sums[j * C : j * C + C, :].astype(BF16)
    mr[b] = ms[b]
    sum_copies = beam_copy(lambda peer: ms.at[peer], mr.at[b], 1)
    start_all(sum_copies, nb)

    sub_e = lax.broadcasted_iota(jnp.int32, (256, 1024), 0)
    src = es[...]
    src_lo = (sub_e == (src & 255)).astype(F32).astype(BF16)
    src_hi = src >> 8
    dst_hot = (sub_e == et[...]).astype(F32).astype(BF16)
    back_agg = mm(cot[...], uw[...], NT).astype(BF16)
    agg_edge = mm(back_agg, dst_hot, TN)

    wait_all(count_copies, nb)
    wait_all(sum_copies, nb)
    total = mr[0].astype(F32)
    number = cr[0]
    for j in range(1, 16):
        total = total + mr[j].astype(F32)
        number = number + cr[j]
    inverse = 1.0 / jnp.maximum(number[0:1, :], 1.0)
    pooled = (total * inverse).astype(BF16)
    pa[b] = pooled
    pool_copies = beam_copy(lambda peer: pa.at[b], pa.at[b], 2)
    start_all(pool_copies, nb)

    pre_own = mm(pooled, emb[...], TN)
    silu_own, slope_own = sig_parts(pre_own)
    own = silu_own.astype(BF16)
    back_self = mm(emb[...], (cot[...].astype(F32) * slope_own).astype(BF16), NT)

    wait_all(pool_copies, nb)
    table = pa[...].reshape(16 * C, 256)
    picked = jnp.zeros((C, 1024), F32)
    every = mm(table, src_lo, NN)
    for q in range(16):
        picked = jnp.where(src_hi == q, every[q * C : q * C + C, :], picked)
    pre_src = mm(emb[...], picked.astype(BF16), TN)
    silu_src, slope_src = sig_parts(pre_src)
    pre_msg = mm(mw[...], silu_src.astype(BF16), TN)
    silu_msg, slope_msg = sig_parts(pre_msg)
    back_pre = (agg_edge * slope_msg).astype(BF16)
    back_src = mm(mw[...], back_pre, NN)
    back_edge = mm(emb[...], (back_src * slope_src).astype(BF16), NN)
    for q in range(16):
        ahot[q * C : q * C + C, :] = jnp.where(src_hi == q, back_edge, 0.0).astype(BF16)
    back_sums = mm(ahot[...], src_lo, NT)
    for j in range(16):
        ms2[j] = back_sums[j * C : j * C + C, :].astype(BF16)
    mr2[b] = ms2[b]
    back_copies = beam_copy(lambda peer: ms2.at[peer], mr2.at[b], 3)
    start_all(back_copies, nb)

    gathered = mm(dst_hot, silu_msg.astype(BF16), NT).astype(BF16)
    fo[...] = (own.astype(F32) + mm(gathered, uw[...], NN)).astype(BF16)

    wait_all(back_copies, nb)
    remote = back_self
    for j in range(16):
        remote = remote + mr2[j].astype(F32)
    bm[b] = (remote * inverse).astype(BF16)
    mean_copies = beam_copy(lambda peer: bm.at[b], bm.at[b], 4)
    start_all(mean_copies, nb)
    wait_all(mean_copies, nb)

    def backward(x, carry):
        ids = fids(x)
        means = bm[...].reshape(16 * C, 256)
        for k in range(2):
            g = 2 * x + k
            for yo in range(YB):
                r = k * YB + yo
                hi = ids[r : r + 1, :] >> 8
                res[...] = mm(means, lohot[g, :, yo * 256 : yo * 256 + 256], NN)
                hid = res[0:C, :]
                for q in range(1, 16):
                    hid = jnp.where(hi == q, res[q * C : q * C + C, :], hid)
                bh[g, yo * C : yo * C + C, :] = hid.astype(BF16)
                back = hid * slopes[g, yo * C : yo * C + C, :]
                bc[g, yo * C : yo * C + C, :] = back.astype(BF16)
                for h in range(2):
                    y = 8 * h + YB * k + yo
                    tile = back[:, h * 128 : h * 128 + 128]
                    plain[1, x, y * C : y * C + C, :] = tile.astype(BF16)
                    spread(gcols, x + 1, y + 1, tile, lane)
        return carry

    lax.fori_loop(0, 8, backward, 0)
    back_halos = halo_copies(plain.at[1], gx, gy, gcn, 8)
    for copy in back_halos:
        copy.start()

    gbig[...] = jnp.zeros_like(gbig)

    def weights(x, carry):
        for k in range(2):
            start = pl.multiple_of(x * WIN, C)
            gbig[...] += mm(bc[2 * x + k], cols[k, pl.ds(start, KC), :], NT)
        return carry

    lax.fori_loop(0, 8, weights, 0)
    gs[...] = jnp.zeros_like(gs)
    for a in range(3):
        part = gbig[0:C, a * WIN : a * WIN + 288]
        for yo in range(1, YB):
            at = a * WIN + yo * 96
            part = part + gbig[yo * C : yo * C + C, at : at + 288]
        gs[:, a * 288 : a * 288 + 288] = part
    for r in range(4):
        for l in range(4):
            g2s[4 * r + l] = gs[r * 8 : r * 8 + 8, l * 256 : l * 256 + 256]
    g1[b] = g2s[b]
    first = beam_copy(lambda peer: g2s.at[peer], g1.at[b], 5)
    start_all(first, nb)

    for copy in back_halos:
        copy.wait()
    place_halos(gcols, gx, gy, gcn)

    def conv_back(x, carry):
        for k in range(2):
            g = 2 * x + k
            start = pl.multiple_of(x * WIN, C)
            conv = mm(gwide[...], gcols[k, pl.ds(start, KC), :], NN)
            full = mrow * (conv + bh[g].astype(F32))
            for yo in range(YB):
                for h in range(2):
                    y = 8 * h + YB * k + yo
                    gf[x, pl.ds(y, C, stride=16), :] = full[
                        yo * C : yo * C + C, h * 128 : h * 128 + 128
                    ]
        return carry

    lax.fori_loop(0, 3, conv_back, 0)
    wait_all(first, nb)
    part = g1[0]
    for j in range(1, 16):
        part = part + g1[j]
    g2[d] = part
    second = drift_copy(g2.at[d], g2.at[d])
    start_all(second, nd)
    lax.fori_loop(3, 6, conv_back, 0)
    wait_all(second, nd)
    part = g2[0]
    for j in range(1, 8):
        part = part + g2[j]
    g3[b] = part
    third = beam_copy(lambda peer: g3.at[b], g3.at[b], 6)
    start_all(third, nb)
    lax.fori_loop(6, 8, conv_back, 0)
    wait_all(third, nb)
    for r in range(4):
        for l in range(4):
            gs[r * 8 : r * 8 + 8, l * 256 : l * 256 + 256] = g3[4 * r + l]
    gc[...] = gs[:, 0:864]


def body(nd, nb, features, occupied, fragments, cw, emb, mw, uw, es, et, cot):
    flipped = cw.reshape(C, 27, C)[:, ::-1, :].transpose(2, 1, 0).reshape(C, 27 * C)
    vmem = pl.BlockSpec(memory_space=pltpu.VMEM)
    scratch = [
        pltpu.VMEM((512, 128), F32),
        pltpu.VMEM((2, 8, 512, 128), BF16),
        pltpu.VMEM((2, 10 * WIN, 256), BF16),
        pltpu.VMEM((2, 10 * WIN, 256), BF16),
        pltpu.VMEM((YB * C, KC), BF16),
        pltpu.VMEM((YB * C, KC), BF16),
        pltpu.VMEM((16, 256, 1024), BF16),
        pltpu.VMEM((512, 1024), BF16),
        pltpu.VMEM((16, YB * C, 256), F32),
        pltpu.VMEM((16, YB * C, 256), BF16),
        pltpu.VMEM((16, YB * C, 256), BF16),
        pltpu.VMEM((512, 256), F32),
        pltpu.VMEM((512, 256), F32),
        pltpu.VMEM((YB * C, KC), F32),
        pltpu.VMEM((2, 512, 128), BF16),
        pltpu.VMEM((2, 8, C, 128), BF16),
        pltpu.VMEM((4, C, 128), BF16),
        pltpu.VMEM((2, 512, 128), BF16),
        pltpu.VMEM((2, 8, C, 128), BF16),
        pltpu.VMEM((4, C, 128), BF16),
        pltpu.VMEM((nb, 8, 256), F32),
        pltpu.VMEM((nb, 8, 256), F32),
        pltpu.VMEM((nb, C, 256), BF16),
        pltpu.VMEM((nb, C, 256), BF16),
        pltpu.VMEM((nb, C, 256), BF16),
        pltpu.VMEM((nb, C, 256), BF16),
        pltpu.VMEM((nb, C, 256), BF16),
        pltpu.VMEM((nb, C, 256), BF16),
        pltpu.VMEM((C, 1024), F32),
        pltpu.VMEM((nb, 8, 256), F32),
        pltpu.VMEM((nb, 8, 256), F32),
        pltpu.VMEM((nd, 8, 256), F32),
        pltpu.VMEM((nb, 8, 256), F32),
        pltpu.SemaphoreType.DMA((16,)),
        pltpu.SemaphoreType.DMA((16,)),
        pltpu.SemaphoreType.DMA((7, nb)),
        pltpu.SemaphoreType.DMA((7, nb)),
        pltpu.SemaphoreType.DMA((nd,)),
        pltpu.SemaphoreType.DMA((nd,)),
    ]
    fo, gf, gc = pl.pallas_call(
        functools.partial(kernel, nd, nb),
        out_shape=(
            jax.ShapeDtypeStruct((256, 256), BF16),
            jax.ShapeDtypeStruct((8, 512, 128), F32),
            jax.ShapeDtypeStruct((C, 27 * C), F32),
        ),
        in_specs=[vmem] * 11,
        out_specs=(vmem, vmem, vmem),
        scratch_shapes=scratch,
        compiler_params=pltpu.CompilerParams(
            collective_id=0, has_side_effects=True, vmem_limit_bytes=60 << 20
        ),
    )(
        features.reshape(8, 512, 128),
        occupied.reshape(2, 16),
        fragments,
        cw,
        flipped,
        emb,
        mw,
        uw,
        es.reshape(1, -1),
        et.reshape(1, -1),
        cot,
    )
    return fo, gf.reshape(8, C, 16, 128), gc


def solution(mesh):
    return jax.shard_map(
        functools.partial(body, mesh.shape["drift"], mesh.shape["beam"]),
        mesh=mesh,
        in_specs=(
            P("drift", None, "beam", None),
            P("drift", "beam", None),
            P("drift", "beam", None),
            P(),
            P(),
            P(),
            P(),
            P(("drift", "beam")),
            P(("drift", "beam")),
            P(("drift", "beam"), None),
        ),
        out_specs=(P(("drift", "beam"), None), P("drift", None, "beam", None), P()),
        check_vma=False,
    )
```

```python
import functools

import jax
import jax.numpy as jnp
from jax import lax
from jax.experimental import pallas as pl
from jax.experimental.pallas import tpu as pltpu
from jax.sharding import PartitionSpec as P

F32 = jnp.float32
BF16 = jnp.bfloat16
MESH = pl.DeviceIdType.MESH
C = 32
YB = 4
WIN = (YB + 2) * 3 * C
KC = 3 * WIN
NN = (((1,), (0,)), ((), ()))
NT = (((1,), (1,)), ((), ()))
TN = (((0,), (0,)), ((), ()))


def mm(lhs, rhs, dims):
    return lax.dot_general(lhs, rhs, dims, preferred_element_type=F32)


def sig_parts(value):
    sig = 1.0 / (1.0 + jnp.exp(-value))
    return value * sig, sig * (1.0 + value * (1.0 - sig))


def spread(cols, x, row, tile, lane):
    left = jnp.where(lane == 0, 0.0, pltpu.roll(tile, 1, 1)).astype(BF16)
    right = jnp.where(lane == 127, 0.0, pltpu.roll(tile, 127, 1)).astype(BF16)
    mid = tile.astype(BF16)
    for half in range(2):
        for k in range(2):
            inner = row - 8 * half - 4 * k
            if 0 <= inner < YB + 2:
                for tap, part in enumerate((left, mid, right)):
                    start = pl.multiple_of(x * WIN + inner * 96 + tap * C, C)
                    at = k * 256 + half * 128
                    cols[pl.ds(start, C), at : at + 128] = part


def widen(wide, weight):
    wide[...] = jnp.zeros_like(wide)
    for yo in range(YB):
        for a in range(3):
            at = a * WIN + yo * 96
            wide[yo * C : yo * C + C, at : at + 288] = weight[:, a * 288 : a * 288 + 288].astype(BF16)


def kernel(
    nd,
    nb,
    feat_in,
    occ_in,
    vf_in,
    cw_in,
    emb_in,
    mw_in,
    uw_in,
    es_in,
    et_in,
    cot_in,
    fo,
    gf,
    gc,
    feat,
    occ,
    vf,
    cw,
    emb,
    mw,
    uw,
    es,
    et,
    cot,
    in_sem,
    stage,
    flip,
    plain,
    cols,
    gcols,
    wide,
    gwide,
    lohot,
    ahot,
    ahot1,
    slopes,
    bh,
    bc,
    bc1,
    res,
    sums,
    gbig,
    hx,
    hy,
    hc,
    gx,
    gy,
    gcn,
    cs,
    cr,
    ms,
    mr,
    pa,
    ms2,
    mr2,
    bm,
    gs,
    g1,
    g2s,
    g2,
    g3,
    hs,
    hr,
    ks,
    kr,
    ps,
    pr,
):
    d = lax.axis_index("drift")
    b = lax.axis_index("beam")
    dn, dp = lax.rem(d + 1, nd), lax.rem(d + nd - 1, nd)
    bn, bp = lax.rem(b + 1, nb), lax.rem(b + nb - 1, nb)

    loads = [
        pltpu.make_async_copy(src, dst, in_sem.at[i])
        for i, (src, dst) in enumerate(
            (
                (occ_in, occ),
                (feat_in, feat),
                (cw_in, cw),
                (vf_in, vf),
                (emb_in, emb),
                (mw_in, mw),
                (uw_in, uw),
                (es_in, es),
                (et_in, et),
                (cot_in, cot),
            )
        )
    ]
    for copy in loads:
        copy.start()
    barrier = pltpu.get_barrier_semaphore()

    def greet(dev):
        pl.semaphore_signal(barrier, inc=1, device_id=dev, device_id_type=MESH)

    def greet_beam(off, carry):
        greet((d, lax.rem(b + off, nb)))
        return carry

    def greet_drift(off, carry):
        greet((lax.rem(d + off, nd), b))
        return carry

    lax.fori_loop(1, nb, greet_beam, 0)
    lax.fori_loop(1, nd, greet_drift, 0)
    for dev in ((dn, bn), (dn, bp), (dp, bn), (dp, bp)):
        greet(dev)
    for copy in loads:
        copy.wait()

    lane = lax.broadcasted_iota(jnp.int32, (C, 128), 1)
    square = (C, C)
    eye = (
        lax.broadcasted_iota(jnp.int32, square, 0) == lax.broadcasted_iota(jnp.int32, square, 1)
    ).astype(F32).astype(BF16)
    group = lax.broadcasted_iota(jnp.int32, (1, 128), 1) // 8
    occ_f = occ[...].astype(F32)
    rows = []
    for j in range(2):
        row = jnp.zeros((1, 128), F32)
        for q in range(16):
            row = jnp.where(group == q, occ_f[j : j + 1, q : q + 1], row)
        rows.append(row)
    mrow = jnp.concatenate(rows, axis=1)
    x_lo = jnp.where(d > 0, 1.0, 0.0).astype(F32)
    x_hi = jnp.where(d < nd - 1, 1.0, 0.0).astype(F32)
    y_lo = jnp.where(b > 0, 1.0, 0.0).astype(F32)
    y_hi = jnp.where(b < nb - 1, 1.0, 0.0).astype(F32)

    def halo_copies(src, tx, ty, tc, base):
        plan = (
            (src.at[7], tx.at[0], (dn, b)),
            (src.at[0], tx.at[1], (dp, b)),
            (src.at[:, 480:512, :], ty.at[0], (d, bn)),
            (src.at[:, 0:32, :], ty.at[1], (d, bp)),
            (src.at[7, 480:512, :], tc.at[0], (dn, bn)),
            (src.at[7, 0:32, :], tc.at[1], (dn, bp)),
            (src.at[0, 480:512, :], tc.at[2], (dp, bn)),
            (src.at[0, 0:32, :], tc.at[3], (dp, bp)),
        )
        return [
            pltpu.make_async_remote_copy(
                src_ref=s,
                dst_ref=t,
                send_sem=hs.at[base + i],
                recv_sem=hr.at[base + i],
                device_id=dev,
                device_id_type=MESH,
            )
            for i, (s, t, dev) in enumerate(plan)
        ]

    def place_halos(target, tx, ty, tc):
        for y in range(16):
            spread(target, 0, y + 1, tx[0, y * C : y * C + C, :].astype(F32) * x_lo, lane)
            spread(target, 9, y + 1, tx[1, y * C : y * C + C, :].astype(F32) * x_hi, lane)

        def per_x(x, carry):
            spread(target, x + 1, 0, ty[0, x].astype(F32) * y_lo, lane)
            spread(target, x + 1, 17, ty[1, x].astype(F32) * y_hi, lane)
            return carry

        lax.fori_loop(0, 8, per_x, 0)
        spread(target, 0, 0, tc[0].astype(F32) * (x_lo * y_lo), lane)
        spread(target, 0, 17, tc[1].astype(F32) * (x_lo * y_hi), lane)
        spread(target, 9, 0, tc[2].astype(F32) * (x_hi * y_lo), lane)
        spread(target, 9, 17, tc[3].astype(F32) * (x_hi * y_hi), lane)

    by, bz = lax.rem(b, 4), b // 4
    far = sorted(range(1, 16), key=lambda o: -(min(o % 4, 4 - o % 4) + min(o // 4, 4 - o // 4)))

    def beam_copy(src, dst, base):
        def make(off):
            peer = 4 * lax.rem(bz + off // 4, 4) + lax.rem(by + off % 4, 4)
            return pltpu.make_async_remote_copy(
                src_ref=src(peer),
                dst_ref=dst,
                send_sem=ks.at[base, off],
                recv_sem=kr.at[base, off],
                device_id=(d, peer),
                device_id_type=MESH,
            )

        return make

    def drift_copy(src, dst, base):
        def make(off):
            peer = lax.rem(d + off, nd)
            return pltpu.make_async_remote_copy(
                src_ref=src(peer),
                dst_ref=dst,
                send_sem=ps.at[base, off],
                recv_sem=pr.at[base, off],
                device_id=(peer, b),
                device_id_type=MESH,
            )

        return make

    def start_all(make, count):
        for off in far if count == nb else range(1, count):
            make(off).start()

    def wait_all(make, count):
        for off in range(1, count):
            make(off).wait()

    def load_row(x, carry):
        stage[...] = feat[x].astype(F32)
        for y in range(16):
            h = y // 8
            tile = stage[pl.ds(y, C, stride=16), :] * mrow[:, h * 128 : h * 128 + 128]
            plain[0, x, y * C : y * C + C, :] = tile.astype(BF16)
            spread(cols, x + 1, y + 1, tile, lane)
        return carry

    lax.fori_loop(0, 8, load_row, 0)
    widen(wide, cw)
    turned = mm(cw[...], eye, TN)
    for t in range(27):
        flip[:, (26 - t) * C : (27 - t) * C] = turned[t * C : t * C + C, :]
    widen(gwide, flip)
    pl.semaphore_wait(barrier, nb - 1 + nd - 1 + 4)
    halos = halo_copies(plain.at[0], hx, hy, hc, 0)
    for copy in halos:
        copy.start()

    sub_hi = lax.broadcasted_iota(jnp.int32, (16, 256), 0)
    sub_b = sub_hi.astype(F32).astype(BF16)
    one_b = jnp.ones((16, 256), BF16)
    zero_b = jnp.zeros((16, 256), BF16)

    def fids(x):
        return jnp.concatenate([vf[x, 0:8, :], vf[x, 8:16, :]], axis=1)

    def counts_of(x, total):
        ids = fids(x)
        for k in range(2):
            parts = []
            for yo in range(YB):
                r = k * YB + yo
                one = ids[r : r + 1, :]
                lo = one & 255
                hi = one >> 8
                lo_b = jnp.broadcast_to(lo, (16, 256)).astype(F32).astype(BF16)
                for j in range(16):
                    lohot[2 * x + k, j * 16 : j * 16 + 16, yo * 256 : yo * 256 + 256] = jnp.where(
                        sub_b == lo_b - BF16(16 * j), one_b, zero_b
                    )
                parts.append(jnp.where(sub_hi == hi, mrow, 0.0).astype(BF16))
            total = total + mm(jnp.concatenate(parts, axis=1), lohot[2 * x + k], NT)
        return total

    counts = lax.fori_loop(0, 8, counts_of, jnp.zeros((16, 256), F32))
    for j in range(16):
        cs[j] = jnp.broadcast_to(counts[j : j + 1, :], (8, 256))
    cr[b] = cs[b]
    count_copies = beam_copy(lambda peer: cs.at[peer], cr.at[b], 0)
    start_all(count_copies, nb)

    for copy in halos:
        copy.wait()
    place_halos(cols, hx, hy, hc)

    sums[...] = jnp.zeros_like(sums)

    zero_h = jnp.zeros((C, 256), BF16)

    def convolve(x, k, hot):
        ids = fids(x)
        start = pl.multiple_of(x * WIN, C)
        conv = mm(wide[...], cols[pl.ds(start, KC), k * 256 : k * 256 + 256], NN)
        slopes[2 * x + k] = conv
        silu = conv / (1.0 + jnp.exp(-conv))
        for yo in range(YB):
            at = pl.multiple_of((x + 1) * WIN + (yo + 1) * 96 + C, C)
            act = cols[pl.ds(at, C), k * 256 : k * 256 + 256].astype(F32)
            hid = (mrow * (act + silu[yo * C : yo * C + C, :])).astype(BF16)
            r = k * YB + yo
            hi = jnp.broadcast_to(ids[r : r + 1, :] >> 8, (C, 256)).astype(F32).astype(BF16)
            for q in range(16):
                hot[q * C : q * C + C, yo * 256 : yo * 256 + 256] = jnp.where(
                    hi == BF16(q), hid, zero_h
                )

    def scatter(g, hot):
        sums[...] += mm(hot[...], lohot[g], NT)

    def forward(x, carry):
        scatter(2 * x, ahot)
        convolve(x, 1, ahot1)
        scatter(2 * x + 1, ahot1)
        convolve(x + 1, 0, ahot)
        return carry

    convolve(0, 0, ahot)
    lax.fori_loop(0, 7, forward, 0)
    scatter(14, ahot)
    convolve(7, 1, ahot1)
    scatter(15, ahot1)
    for j in range(16):
        ms[j] = sums[j * C : j * C + C, :].astype(BF16)
    mr[b] = ms[b]
    sum_copies = beam_copy(lambda peer: ms.at[peer], mr.at[b], 1)
    start_all(sum_copies, nb)

    def slope_of(g, carry):
        sig = 1.0 / (1.0 + jnp.exp(-slopes[g]))
        slopes[g] = mrow * (sig * (1.0 + slopes[g] * (1.0 - sig)))
        return carry

    lax.fori_loop(0, 16, slope_of, 0)

    sub_e = lax.broadcasted_iota(jnp.int32, (256, 1024), 0)
    src = es[...]
    src_lo = (sub_e == (src & 255)).astype(F32).astype(BF16)
    src_hi = src >> 8
    dst_hot = (sub_e == et[...]).astype(F32).astype(BF16)
    back_agg = mm(cot[...], uw[...], NT).astype(BF16)
    agg_edge = mm(back_agg, dst_hot, TN)

    wait_all(count_copies, nb)
    wait_all(sum_copies, nb)
    total = mr[0].astype(F32)
    number = cr[0]
    for j in range(1, 16):
        total = total + mr[j].astype(F32)
        number = number + cr[j]
    inverse = 1.0 / jnp.maximum(number[0:1, :], 1.0)
    pooled = (total * inverse).astype(BF16)
    pa[b] = pooled
    pool_copies = beam_copy(lambda peer: pa.at[b], pa.at[b], 2)
    start_all(pool_copies, nb)

    pre_own = mm(pooled, emb[...], TN)
    silu_own, slope_own = sig_parts(pre_own)
    own = silu_own.astype(BF16)
    back_self = mm(emb[...], (cot[...].astype(F32) * slope_own).astype(BF16), NT)

    wait_all(pool_copies, nb)
    table = pa[...].reshape(16 * C, 256)
    picked = jnp.zeros((C, 1024), F32)
    every = mm(table, src_lo, NN)
    for q in range(16):
        picked = jnp.where(src_hi == q, every[q * C : q * C + C, :], picked)
    pre_src = mm(emb[...], picked.astype(BF16), TN)
    silu_src, slope_src = sig_parts(pre_src)
    pre_msg = mm(mw[...], silu_src.astype(BF16), TN)
    silu_msg, slope_msg = sig_parts(pre_msg)
    back_pre = (agg_edge * slope_msg).astype(BF16)
    back_src = mm(mw[...], back_pre, NN)
    back_edge = mm(emb[...], (back_src * slope_src).astype(BF16), NN)
    for q in range(16):
        ahot[q * C : q * C + C, :] = jnp.where(src_hi == q, back_edge, 0.0).astype(BF16)
    back_sums = mm(ahot[...], src_lo, NT)
    for j in range(16):
        ms2[j] = back_sums[j * C : j * C + C, :].astype(BF16)
    mr2[b] = ms2[b]
    back_copies = beam_copy(lambda peer: ms2.at[peer], mr2.at[b], 3)
    start_all(back_copies, nb)

    gathered = mm(dst_hot, silu_msg.astype(BF16), NT).astype(BF16)
    fo[...] = (own.astype(F32) + mm(gathered, uw[...], NN)).astype(BF16)

    wait_all(back_copies, nb)
    remote = back_self
    for j in range(16):
        remote = remote + mr2[j].astype(F32)
    bm[b] = (remote * inverse).astype(BF16)
    mean_copies = beam_copy(lambda peer: bm.at[b], bm.at[b], 4)
    start_all(mean_copies, nb)
    wait_all(mean_copies, nb)

    def spread_means(x, out):
        ids = fids(x)
        means = bm[...].reshape(16 * C, 256)
        for k in range(2):
            g = 2 * x + k
            for yo in range(YB):
                r = k * YB + yo
                hi = ids[r : r + 1, :] >> 8
                res[...] = mm(means, lohot[g, :, yo * 256 : yo * 256 + 256], NN)
                hid = res[0:C, :]
                for q in range(1, 16):
                    hid = jnp.where(hi == q, res[q * C : q * C + C, :], hid)
                bh[g, yo * C : yo * C + C, :] = hid.astype(BF16)
                back = hid * slopes[g, yo * C : yo * C + C, :]
                out[yo * C : yo * C + C, k * 256 : k * 256 + 256] = back.astype(BF16)
                for h in range(2):
                    y = 8 * h + YB * k + yo
                    tile = back[:, h * 128 : h * 128 + 128]
                    plain[1, x, y * C : y * C + C, :] = tile.astype(BF16)
                    spread(gcols, x + 1, y + 1, tile, lane)

    gbig[...] = jnp.zeros_like(gbig)

    def weights(x, back):
        start = pl.multiple_of(x * WIN, C)
        gbig[...] += mm(back[...], cols[pl.ds(start, KC), :], NT)

    def backward(i, carry):
        weights(2 * i, bc)
        spread_means(2 * i + 1, bc1)
        weights(2 * i + 1, bc1)
        spread_means(2 * i + 2, bc)
        return carry

    spread_means(0, bc)
    lax.fori_loop(0, 3, backward, 0)
    weights(6, bc)
    spread_means(7, bc1)
    back_halos = halo_copies(plain.at[1], gx, gy, gcn, 8)
    for copy in back_halos:
        copy.start()
    weights(7, bc1)
    gs[...] = jnp.zeros_like(gs)
    for a in range(3):
        part = gbig[0:C, a * WIN : a * WIN + 288]
        for yo in range(1, YB):
            at = a * WIN + yo * 96
            part = part + gbig[yo * C : yo * C + C, at : at + 288]
        gs[:, a * 288 : a * 288 + 288] = part
    for r in range(2):
        for l in range(4):
            g2s[4 * r + l] = gs[r * 16 : r * 16 + 16, l * 256 : l * 256 + 256]
    g1[d] = g2s[d]
    first = drift_copy(lambda peer: g2s.at[peer], g1.at[d], 0)
    start_all(first, nd)

    def conv_back(x, carry):
        for k in range(2):
            g = 2 * x + k
            start = pl.multiple_of(x * WIN, C)
            conv = mm(gwide[...], gcols[pl.ds(start, KC), k * 256 : k * 256 + 256], NN)
            full = mrow * (conv + bh[g].astype(F32))
            for yo in range(YB):
                for h in range(2):
                    y = 8 * h + YB * k + yo
                    gf[x, pl.ds(y, C, stride=16), :] = full[
                        yo * C : yo * C + C, h * 128 : h * 128 + 128
                    ]
        return carry

    wait_all(first, nd)
    part = g1[0]
    for j in range(1, 8):
        part = part + g1[j]
    g2[b] = part.astype(BF16)
    second = beam_copy(lambda peer: g2.at[b], g2.at[b], 5)
    start_all(second, nb)
    for copy in back_halos:
        copy.wait()
    place_halos(gcols, gx, gy, gcn)
    lax.fori_loop(0, 3, conv_back, 0)
    wait_all(second, nb)
    part = g2[0].astype(F32)
    for j in range(1, 16):
        part = part + g2[j].astype(F32)
    g3[d] = part
    third = drift_copy(lambda peer: g3.at[d], g3.at[d], 1)
    start_all(third, nd)
    lax.fori_loop(3, 8, conv_back, 0)
    wait_all(third, nd)
    for r in range(2):
        for l in range(4):
            gs[r * 16 : r * 16 + 16, l * 256 : l * 256 + 256] = g3[4 * r + l]
    gc[...] = gs[:, 0:864]


def store(fo, gf, gc, fo_out, gf_out, gc_out, sem):
    copies = [
        pltpu.make_async_copy(src, dst, sem.at[i])
        for i, (src, dst) in enumerate(((gf, gf_out), (fo, fo_out), (gc, gc_out)))
    ]
    for copy in copies:
        copy.start()
    for copy in copies:
        copy.wait()


def body(nd, nb, features, occupied, fragments, cw, emb, mw, uw, es, et, cot):
    vmem = pl.BlockSpec(memory_space=pltpu.VMEM)
    hbm = pl.BlockSpec(memory_space=pltpu.HBM)
    inputs = (
        features.reshape(8, 512, 128),
        occupied.reshape(2, 16),
        fragments,
        cw,
        emb,
        mw,
        uw,
        es.reshape(1, -1),
        et.reshape(1, -1),
        cot,
    )
    scratch = [pltpu.VMEM(one.shape, one.dtype) for one in inputs] + [
        pltpu.SemaphoreType.DMA((10,)),
        pltpu.VMEM((512, 128), F32),
        pltpu.VMEM((C, 27 * C), F32),
        pltpu.VMEM((2, 8, 512, 128), BF16),
        pltpu.VMEM((10 * WIN, 512), BF16),
        pltpu.VMEM((10 * WIN, 512), BF16),
        pltpu.VMEM((YB * C, KC), BF16),
        pltpu.VMEM((YB * C, KC), BF16),
        pltpu.VMEM((16, 256, 1024), BF16),
        pltpu.VMEM((512, 1024), BF16),
        pltpu.VMEM((512, 1024), BF16),
        pltpu.VMEM((16, YB * C, 256), F32),
        pltpu.VMEM((16, YB * C, 256), BF16),
        pltpu.VMEM((YB * C, 512), BF16),
        pltpu.VMEM((YB * C, 512), BF16),
        pltpu.VMEM((512, 256), F32),
        pltpu.VMEM((512, 256), F32),
        pltpu.VMEM((YB * C, KC), F32),
        pltpu.VMEM((2, 512, 128), BF16),
        pltpu.VMEM((2, 8, C, 128), BF16),
        pltpu.VMEM((4, C, 128), BF16),
        pltpu.VMEM((2, 512, 128), BF16),
        pltpu.VMEM((2, 8, C, 128), BF16),
        pltpu.VMEM((4, C, 128), BF16),
        pltpu.VMEM((nb, 8, 256), F32),
        pltpu.VMEM((nb, 8, 256), F32),
        pltpu.VMEM((nb, C, 256), BF16),
        pltpu.VMEM((nb, C, 256), BF16),
        pltpu.VMEM((nb, C, 256), BF16),
        pltpu.VMEM((nb, C, 256), BF16),
        pltpu.VMEM((nb, C, 256), BF16),
        pltpu.VMEM((nb, C, 256), BF16),
        pltpu.VMEM((C, 1024), F32),
        pltpu.VMEM((nd, 16, 256), F32),
        pltpu.VMEM((nd, 16, 256), F32),
        pltpu.VMEM((nb, 16, 256), BF16),
        pltpu.VMEM((nd, 16, 256), F32),
        pltpu.SemaphoreType.DMA((16,)),
        pltpu.SemaphoreType.DMA((16,)),
        pltpu.SemaphoreType.DMA((6, nb)),
        pltpu.SemaphoreType.DMA((6, nb)),
        pltpu.SemaphoreType.DMA((2, nd)),
        pltpu.SemaphoreType.DMA((2, nd)),
    ]
    results = pl.pallas_call(
        functools.partial(kernel, nd, nb),
        out_shape=(
            pltpu.VMEM((256, 256), BF16),
            pltpu.VMEM((8, 512, 128), F32),
            pltpu.VMEM((C, 27 * C), F32),
        ),
        in_specs=[hbm] * 10,
        out_specs=(vmem, vmem, vmem),
        scratch_shapes=scratch,
        compiler_params=pltpu.CompilerParams(
            collective_id=0, has_side_effects=True, vmem_limit_bytes=44 << 20
        ),
    )(*[pltpu.with_memory_space_constraint(one, pltpu.HBM) for one in inputs])
    fo, gf, gc = pl.pallas_call(
        store,
        out_shape=tuple(jax.ShapeDtypeStruct(one.shape, one.dtype) for one in results),
        in_specs=[vmem] * 3,
        out_specs=(hbm,) * 3,
        scratch_shapes=[pltpu.SemaphoreType.DMA((3,))],
        compiler_params=pltpu.CompilerParams(vmem_limit_bytes=1 << 20),
    )(*results)
    return fo, gf.reshape(8, C, 16, 128), gc


def solution(mesh):
    return jax.shard_map(
        functools.partial(body, mesh.shape["drift"], mesh.shape["beam"]),
        mesh=mesh,
        in_specs=(
            P("drift", None, "beam", None),
            P("drift", "beam", None),
            P("drift", "beam", None),
            P(),
            P(),
            P(),
            P(),
            P(("drift", "beam")),
            P(("drift", "beam")),
            P(("drift", "beam"), None),
        ),
        out_specs=(P(("drift", "beam"), None), P("drift", None, "beam", None), P()),
        check_vma=False,
    )
```

```python
import functools

import jax
import jax.numpy as jnp
from jax import lax
from jax.experimental import pallas as pl
from jax.experimental.pallas import tpu as pltpu
from jax.sharding import PartitionSpec as P

F32 = jnp.float32
BF16 = jnp.bfloat16
MESH = pl.DeviceIdType.MESH
C = 32
YB = 4
WIN = (YB + 2) * 3 * C
KC = 3 * WIN
NEAR = 11
NN = (((1,), (0,)), ((), ()))
NT = (((1,), (1,)), ((), ()))
TN = (((0,), (0,)), ((), ()))


def mm(lhs, rhs, dims):
    return lax.dot_general(lhs, rhs, dims, preferred_element_type=F32)


def sig_parts(value):
    sig = 1.0 / (1.0 + jnp.exp(-value))
    return value * sig, sig * (1.0 + value * (1.0 - sig))


def spread(cols, x, row, tile, lane):
    left = jnp.where(lane == 0, 0.0, pltpu.roll(tile, 1, 1)).astype(BF16)
    right = jnp.where(lane == 127, 0.0, pltpu.roll(tile, 127, 1)).astype(BF16)
    mid = tile.astype(BF16)
    for half in range(2):
        for k in range(2):
            inner = row - 8 * half - 4 * k
            if 0 <= inner < YB + 2:
                for tap, part in enumerate((left, mid, right)):
                    start = pl.multiple_of(x * WIN + inner * 96 + tap * C, C)
                    at = k * 256 + half * 128
                    cols[pl.ds(start, C), at : at + 128] = part


def widen(wide, weight):
    wide[...] = jnp.zeros_like(wide)
    for yo in range(YB):
        for a in range(3):
            at = a * WIN + yo * 96
            wide[yo * C : yo * C + C, at : at + 288] = weight[:, a * 288 : a * 288 + 288].astype(BF16)


def kernel(
    nd,
    nb,
    feat_in,
    occ_in,
    vf_in,
    cw_in,
    emb_in,
    mw_in,
    uw_in,
    es_in,
    et_in,
    cot_in,
    fo,
    gf,
    gc,
    feat,
    occ,
    vf,
    cw,
    emb,
    mw,
    uw,
    es,
    et,
    cot,
    in_sem,
    stage,
    flip,
    plain,
    cols,
    gcols,
    wide,
    gwide,
    lohot,
    ahot,
    ahot1,
    slopes,
    bh,
    bc,
    bc1,
    res,
    sums,
    gbig,
    hx,
    hy,
    hc,
    gx,
    gy,
    gcn,
    cs,
    cr,
    ms,
    mr,
    pa,
    ms2,
    mr2,
    bm,
    gs,
    g1,
    g2s,
    g2,
    g3,
    hs,
    hr,
    ks,
    kr,
    ps,
    pr,
):
    d = lax.axis_index("drift")
    b = lax.axis_index("beam")
    dn, dp = lax.rem(d + 1, nd), lax.rem(d + nd - 1, nd)
    bn, bp = lax.rem(b + 1, nb), lax.rem(b + nb - 1, nb)

    loads = [
        pltpu.make_async_copy(src, dst, in_sem.at[i])
        for i, (src, dst) in enumerate(
            (
                (occ_in, occ),
                (feat_in, feat),
                (cw_in, cw),
                (vf_in, vf),
                (emb_in, emb),
                (mw_in, mw),
                (uw_in, uw),
                (es_in, es),
                (et_in, et),
                (cot_in, cot),
            )
        )
    ]
    barrier = pltpu.get_barrier_semaphore()

    def greet(dev):
        pl.semaphore_signal(barrier, inc=1, device_id=dev, device_id_type=MESH)

    def greet_beam(off, carry):
        greet((d, lax.rem(b + off, nb)))
        return carry

    def greet_drift(off, carry):
        greet((lax.rem(d + off, nd), b))
        return carry

    lax.fori_loop(1, nb, greet_beam, 0)
    lax.fori_loop(1, nd, greet_drift, 0)
    for dev in ((dn, bn), (dn, bp), (dp, bn), (dp, bp)):
        greet(dev)
    for copy in loads:
        copy.start()
    for copy in loads:
        copy.wait()

    lane = lax.broadcasted_iota(jnp.int32, (C, 128), 1)
    square = (C, C)
    eye = (
        lax.broadcasted_iota(jnp.int32, square, 0) == lax.broadcasted_iota(jnp.int32, square, 1)
    ).astype(F32).astype(BF16)
    group = lax.broadcasted_iota(jnp.int32, (1, 128), 1) // 8
    occ_f = occ[...].astype(F32)
    rows = []
    for j in range(2):
        row = jnp.zeros((1, 128), F32)
        for q in range(16):
            row = jnp.where(group == q, occ_f[j : j + 1, q : q + 1], row)
        rows.append(row)
    mrow = jnp.concatenate(rows, axis=1)
    x_lo = jnp.where(d > 0, 1.0, 0.0).astype(F32)
    x_hi = jnp.where(d < nd - 1, 1.0, 0.0).astype(F32)
    y_lo = jnp.where(b > 0, 1.0, 0.0).astype(F32)
    y_hi = jnp.where(b < nb - 1, 1.0, 0.0).astype(F32)

    def halo_copies(src, tx, ty, tc, base):
        plan = (
            (src.at[7, 480:512, :], tc.at[0], (dn, bn)),
            (src.at[7, 0:32, :], tc.at[1], (dn, bp)),
            (src.at[0, 480:512, :], tc.at[2], (dp, bn)),
            (src.at[0, 0:32, :], tc.at[3], (dp, bp)),
            (src.at[:, 480:512, :], ty.at[0], (d, bn)),
            (src.at[:, 0:32, :], ty.at[1], (d, bp)),
            (src.at[7], tx.at[0], (dn, b)),
            (src.at[0], tx.at[1], (dp, b)),
        )
        return [
            pltpu.make_async_remote_copy(
                src_ref=s,
                dst_ref=t,
                send_sem=hs.at[base + i],
                recv_sem=hr.at[base + i],
                device_id=dev,
                device_id_type=MESH,
            )
            for i, (s, t, dev) in enumerate(plan)
        ]

    def place_halos(target, tx, ty, tc):
        for y in range(16):
            spread(target, 0, y + 1, tx[0, y * C : y * C + C, :].astype(F32) * x_lo, lane)
            spread(target, 9, y + 1, tx[1, y * C : y * C + C, :].astype(F32) * x_hi, lane)

        def per_x(x, carry):
            spread(target, x + 1, 0, ty[0, x].astype(F32) * y_lo, lane)
            spread(target, x + 1, 17, ty[1, x].astype(F32) * y_hi, lane)
            return carry

        lax.fori_loop(0, 8, per_x, 0)
        spread(target, 0, 0, tc[0].astype(F32) * (x_lo * y_lo), lane)
        spread(target, 0, 17, tc[1].astype(F32) * (x_lo * y_hi), lane)
        spread(target, 9, 0, tc[2].astype(F32) * (x_hi * y_lo), lane)
        spread(target, 9, 17, tc[3].astype(F32) * (x_hi * y_hi), lane)

    by, bz = lax.rem(b, 4), b // 4
    near = sorted(range(16), key=lambda o: min(o % 4, 4 - o % 4) + min(o // 4, 4 - o // 4))
    far = near[:0:-1]
    owner = [4 * lax.rem(bz + 4 - o // 4, 4) + lax.rem(by + 4 - o % 4, 4) for o in near]

    def beam_copy(src, dst, base):
        def make(off):
            peer = 4 * lax.rem(bz + off // 4, 4) + lax.rem(by + off % 4, 4)
            return pltpu.make_async_remote_copy(
                src_ref=src(peer),
                dst_ref=dst(off) if callable(dst) else dst,
                send_sem=ks.at[base, off],
                recv_sem=kr.at[base, off],
                device_id=(d, peer),
                device_id_type=MESH,
            )

        return make

    def drift_copy(src, dst, base):
        def make(off):
            peer = lax.rem(d + off, nd)
            return pltpu.make_async_remote_copy(
                src_ref=src(peer),
                dst_ref=dst,
                send_sem=ps.at[base, off],
                recv_sem=pr.at[base, off],
                device_id=(peer, b),
                device_id_type=MESH,
            )

        return make

    def start_all(make, count):
        for off in far if count == nb else range(1, count):
            make(off).start()

    def wait_all(make, count):
        for off in range(1, count):
            make(off).wait()

    def load_row(x, carry):
        stage[...] = feat[x].astype(F32)
        for y in range(16):
            h = y // 8
            tile = stage[pl.ds(y, C, stride=16), :] * mrow[:, h * 128 : h * 128 + 128]
            plain[0, x, y * C : y * C + C, :] = tile.astype(BF16)
            spread(cols, x + 1, y + 1, tile, lane)
        return carry

    lax.fori_loop(0, 8, load_row, 0)
    pl.semaphore_wait(barrier, nb - 1 + nd - 1 + 4)
    halos = halo_copies(plain.at[0], hx, hy, hc, 0)
    for copy in halos:
        copy.start()

    sub_hi = lax.broadcasted_iota(jnp.int32, (16, 256), 0)
    sub_b = sub_hi.astype(F32).astype(BF16)
    one_b = jnp.ones((16, 256), BF16)
    zero_b = jnp.zeros((16, 256), BF16)

    def fids(x):
        return jnp.concatenate([vf[x, 0:8, :], vf[x, 8:16, :]], axis=1)

    def counts_of(x, total):
        ids = fids(x)
        for k in range(2):
            parts = []
            for yo in range(YB):
                r = k * YB + yo
                one = ids[r : r + 1, :]
                lo = one & 255
                hi = one >> 8
                lo_b = jnp.broadcast_to(lo, (16, 256)).astype(F32).astype(BF16)
                for j in range(16):
                    lohot[2 * x + k, j * 16 : j * 16 + 16, yo * 256 : yo * 256 + 256] = jnp.where(
                        sub_b == lo_b - BF16(16 * j), one_b, zero_b
                    )
                parts.append(jnp.where(sub_hi == hi, mrow, 0.0).astype(BF16))
            total = total + mm(jnp.concatenate(parts, axis=1), lohot[2 * x + k], NT)
        return total

    counts = lax.fori_loop(0, 8, counts_of, jnp.zeros((16, 256), F32))
    for j in range(16):
        cs[j] = jnp.broadcast_to(counts[j : j + 1, :], (8, 256))
    cr[b] = cs[b]
    count_copies = beam_copy(lambda peer: cs.at[peer], cr.at[b], 0)
    start_all(count_copies, nb)

    widen(wide, cw)
    turned = mm(cw[...], eye, TN)
    for t in range(27):
        flip[:, (26 - t) * C : (27 - t) * C] = turned[t * C : t * C + C, :]
    widen(gwide, flip)
    for copy in halos:
        copy.wait()
    place_halos(cols, hx, hy, hc)

    sums[...] = jnp.zeros_like(sums)

    zero_h = jnp.zeros((C, 256), BF16)

    def convolve(x, k, hot):
        ids = fids(x)
        start = pl.multiple_of(x * WIN, C)
        conv = mm(wide[...], cols[pl.ds(start, KC), k * 256 : k * 256 + 256], NN)
        slopes[2 * x + k] = conv
        silu = conv / (1.0 + jnp.exp(-conv))
        for yo in range(YB):
            at = pl.multiple_of((x + 1) * WIN + (yo + 1) * 96 + C, C)
            act = cols[pl.ds(at, C), k * 256 : k * 256 + 256].astype(F32)
            hid = (mrow * (act + silu[yo * C : yo * C + C, :])).astype(BF16)
            r = k * YB + yo
            hi = jnp.broadcast_to(ids[r : r + 1, :] >> 8, (C, 256)).astype(F32).astype(BF16)
            for q in range(16):
                hot[q * C : q * C + C, yo * 256 : yo * 256 + 256] = jnp.where(
                    hi == BF16(q), hid, zero_h
                )

    def scatter(g, hot):
        sums[...] += mm(hot[...], lohot[g], NT)

    def forward(x, carry):
        scatter(2 * x, ahot)
        convolve(x, 1, ahot1)
        scatter(2 * x + 1, ahot1)
        convolve(x + 1, 0, ahot)
        return carry

    convolve(0, 0, ahot)
    lax.fori_loop(0, 7, forward, 0)
    scatter(14, ahot)
    convolve(7, 1, ahot1)
    scatter(15, ahot1)
    for j in range(16):
        ms[j] = sums[j * C : j * C + C, :].astype(BF16)
    mr[b] = ms[b]
    sum_copies = beam_copy(lambda peer: ms.at[peer], mr.at[b], 1)
    start_all(sum_copies, nb)

    def slope_of(g, carry):
        sig = 1.0 / (1.0 + jnp.exp(-slopes[g]))
        slopes[g] = mrow * (sig * (1.0 + slopes[g] * (1.0 - sig)))
        return carry

    lax.fori_loop(0, 16, slope_of, 0)

    sub_e = lax.broadcasted_iota(jnp.int32, (256, 1024), 0)
    src = es[...]
    src_lo = (sub_e == (src & 255)).astype(F32).astype(BF16)
    src_hi = src >> 8
    dst_hot = (sub_e == et[...]).astype(F32).astype(BF16)
    back_agg = mm(cot[...], uw[...], NT).astype(BF16)
    agg_edge = mm(back_agg, dst_hot, TN)

    wait_all(count_copies, nb)
    wait_all(sum_copies, nb)
    total = mr[0].astype(F32)
    number = cr[0]
    for j in range(1, 16):
        total = total + mr[j].astype(F32)
        number = number + cr[j]
    inverse = 1.0 / jnp.maximum(number[0:1, :], 1.0)
    pooled = (total * inverse).astype(BF16)
    pa[b] = pooled
    pool_copies = beam_copy(lambda peer: pa.at[b], pa.at[b], 2)
    start_all(pool_copies, nb)

    pre_own = mm(pooled, emb[...], TN)
    silu_own, slope_own = sig_parts(pre_own)
    own = silu_own.astype(BF16)
    back_self = mm(emb[...], (cot[...].astype(F32) * slope_own).astype(BF16), NT)

    wait_all(pool_copies, nb)
    table = pa[...].reshape(16 * C, 256)
    picked = jnp.zeros((C, 1024), F32)
    every = mm(table, src_lo, NN)
    for q in range(16):
        picked = jnp.where(src_hi == q, every[q * C : q * C + C, :], picked)
    pre_src = mm(emb[...], picked.astype(BF16), TN)
    silu_src, slope_src = sig_parts(pre_src)
    pre_msg = mm(mw[...], silu_src.astype(BF16), TN)
    silu_msg, slope_msg = sig_parts(pre_msg)
    back_pre = (agg_edge * slope_msg).astype(BF16)
    back_src = mm(mw[...], back_pre, NN)
    back_edge = mm(emb[...], (back_src * slope_src).astype(BF16), NN)
    for q in range(16):
        ahot[q * C : q * C + C, :] = jnp.where(src_hi == q, back_edge, 0.0).astype(BF16)
    back_sums = mm(ahot[...], src_lo, NT)
    for j in range(16):
        ms2[j] = back_sums[j * C : j * C + C, :].astype(BF16)
    mr2[b] = ms2[b]
    back_copies = beam_copy(lambda peer: ms2.at[peer], mr2.at[b], 3)
    start_all(back_copies, nb)

    gathered = mm(dst_hot, silu_msg.astype(BF16), NT).astype(BF16)
    fo[...] = (own.astype(F32) + mm(gathered, uw[...], NN)).astype(BF16)

    wait_all(back_copies, nb)
    remote = back_self
    for j in range(16):
        remote = remote + mr2[j].astype(F32)
    bm[0] = (remote * inverse).astype(BF16)
    mean_copies = beam_copy(lambda peer: bm.at[0], lambda off: bm.at[near.index(off)], 4)
    start_all(mean_copies, nb)
    gbig[...] = jnp.zeros_like(gbig)
    for off in near[1:NEAR]:
        mean_copies(off).wait()

    def gather_near(x, carry):
        ids = fids(x)
        means = bm[0:NEAR].reshape(NEAR * C, 256)
        for k in range(2):
            for yo in range(YB):
                r = k * YB + yo
                hi = ids[r : r + 1, :] >> 8
                res[0 : NEAR * C, :] = mm(means, lohot[2 * x + k, :, yo * 256 : yo * 256 + 256], NN)
                hid = res[0:C, :]
                for q in range(1, NEAR):
                    hid = jnp.where(hi == owner[q], res[q * C : q * C + C, :], hid)
                bh[2 * x + k, yo * C : yo * C + C, :] = hid.astype(BF16)
        return carry

    lax.fori_loop(0, 8, gather_near, 0)
    for off in near[NEAR:]:
        mean_copies(off).wait()

    def gather_far(i, out):
        means = bm[NEAR:16].reshape((16 - NEAR) * C, 256)
        for j in range(2):
            x = 2 * i + j
            ids = fids(x)
            for k in range(2):
                g = 2 * x + k
                for yo in range(YB):
                    r = k * YB + yo
                    hi = ids[r : r + 1, :] >> 8
                    got = mm(means, lohot[g, :, yo * 256 : yo * 256 + 256], NN)
                    hid = bh[g, yo * C : yo * C + C, :].astype(F32)
                    for q in range(NEAR, 16):
                        at = (q - NEAR) * C
                        hid = jnp.where(hi == owner[q], got[at : at + C, :], hid)
                    bh[g, yo * C : yo * C + C, :] = hid.astype(BF16)
                    back = hid * slopes[g, yo * C : yo * C + C, :]
                    row = j * YB * C + yo * C
                    out[row : row + C, k * 256 : k * 256 + 256] = back.astype(BF16)
                    for h in range(2):
                        y = 8 * h + YB * k + yo
                        tile = back[:, h * 128 : h * 128 + 128]
                        plain[1, x, y * C : y * C + C, :] = tile.astype(BF16)
                        spread(gcols, x + 1, y + 1, tile, lane)

    def weights(i, back):
        start = pl.multiple_of(2 * i * WIN, C)
        gbig[...] += mm(cols[pl.ds(start, 4 * WIN), :], back[...], NT)

    def backward(i, carry):
        weights(i, bc)
        gather_far(i + 1, bc1)
        bc[...] = bc1[...]
        return carry

    gather_far(0, bc)
    lax.fori_loop(0, 3, backward, 0)
    back_halos = halo_copies(plain.at[1], gx, gy, gcn, 8)
    for copy in back_halos:
        copy.start()
    weights(3, bc)
    quarter = lax.broadcasted_iota(jnp.int32, (288, 128), 1) // C
    for a in range(3):
        total = None
        for j in range(2):
            at = (j + a) * WIN
            part = gbig[at : at + 288, j * 128 : j * 128 + 128]
            for yo in range(1, YB):
                down = at + yo * 96
                part = jnp.where(
                    quarter == yo, gbig[down : down + 288, j * 128 : j * 128 + 128], part
                )
            total = part if total is None else total + part
        total = total + pltpu.roll(total, 64, 1)
        gs[a * 288 : a * 288 + 288, :] = total + pltpu.roll(total, 32, 1)
    packed = gs[0:216, :]
    for j in range(1, 4):
        packed = jnp.where(quarter[0:216] == j, gs[j * 216 : j * 216 + 216, :], packed)
    turned = jnp.concatenate([packed, jnp.zeros((40, 128), F32)], axis=0).T
    for j in range(8):
        g2s[j] = turned[j * 16 : j * 16 + 16, :]
    g1[d] = g2s[d]
    first = drift_copy(lambda peer: g2s.at[peer], g1.at[d], 0)
    start_all(first, nd)

    def conv_back(x, carry):
        for k in range(2):
            g = 2 * x + k
            start = pl.multiple_of(x * WIN, C)
            conv = mm(gwide[...], gcols[pl.ds(start, KC), k * 256 : k * 256 + 256], NN)
            full = mrow * (conv + bh[g].astype(F32))
            for yo in range(YB):
                for h in range(2):
                    y = 8 * h + YB * k + yo
                    gf[x, pl.ds(y, C, stride=16), :] = full[
                        yo * C : yo * C + C, h * 128 : h * 128 + 128
                    ]
        return carry

    wait_all(first, nd)
    part = g1[0]
    for j in range(1, 8):
        part = part + g1[j]
    g2[b] = part.astype(BF16)
    second = beam_copy(lambda peer: g2.at[b], g2.at[b], 5)
    start_all(second, nb)
    for copy in back_halos:
        copy.wait()
    place_halos(gcols, gx, gy, gcn)
    lax.fori_loop(0, 3, conv_back, 0)
    wait_all(second, nb)
    part = g2[0].astype(F32)
    for j in range(1, 16):
        part = part + g2[j].astype(F32)
    g3[d] = part
    third = drift_copy(lambda peer: g3.at[d], g3.at[d], 1)
    start_all(third, nd)
    lax.fori_loop(3, 8, conv_back, 0)
    wait_all(third, nd)
    for j in range(8):
        at = (j // 2) * 216
        gc[(j % 2) * 16 : (j % 2) * 16 + 16, at : at + 216] = g3[j, :, 0:216]


def store(fo, gf, gc, fo_out, gf_out, gc_out, sem):
    copies = [
        pltpu.make_async_copy(src, dst, sem.at[i])
        for i, (src, dst) in enumerate(((gf, gf_out), (fo, fo_out), (gc, gc_out)))
    ]
    for copy in copies:
        copy.start()
    for copy in copies:
        copy.wait()


def body(nd, nb, features, occupied, fragments, cw, emb, mw, uw, es, et, cot):
    vmem = pl.BlockSpec(memory_space=pltpu.VMEM)
    hbm = pl.BlockSpec(memory_space=pltpu.HBM)
    inputs = (
        features.reshape(8, 512, 128),
        occupied.reshape(2, 16),
        fragments,
        cw,
        emb,
        mw,
        uw,
        es.reshape(1, -1),
        et.reshape(1, -1),
        cot,
    )
    scratch = [pltpu.VMEM(one.shape, one.dtype) for one in inputs] + [
        pltpu.SemaphoreType.DMA((10,)),
        pltpu.VMEM((512, 128), F32),
        pltpu.VMEM((C, 27 * C), F32),
        pltpu.VMEM((2, 8, 512, 128), BF16),
        pltpu.VMEM((10 * WIN, 512), BF16),
        pltpu.VMEM((10 * WIN, 512), BF16),
        pltpu.VMEM((YB * C, KC), BF16),
        pltpu.VMEM((YB * C, KC), BF16),
        pltpu.VMEM((16, 256, 1024), BF16),
        pltpu.VMEM((512, 1024), BF16),
        pltpu.VMEM((512, 1024), BF16),
        pltpu.VMEM((16, YB * C, 256), F32),
        pltpu.VMEM((16, YB * C, 256), BF16),
        pltpu.VMEM((2 * YB * C, 512), BF16),
        pltpu.VMEM((2 * YB * C, 512), BF16),
        pltpu.VMEM((512, 256), F32),
        pltpu.VMEM((512, 256), F32),
        pltpu.VMEM((4 * WIN, 256), F32),
        pltpu.VMEM((2, 512, 128), BF16),
        pltpu.VMEM((2, 8, C, 128), BF16),
        pltpu.VMEM((4, C, 128), BF16),
        pltpu.VMEM((2, 512, 128), BF16),
        pltpu.VMEM((2, 8, C, 128), BF16),
        pltpu.VMEM((4, C, 128), BF16),
        pltpu.VMEM((nb, 8, 256), F32),
        pltpu.VMEM((nb, 8, 256), F32),
        pltpu.VMEM((nb, C, 256), BF16),
        pltpu.VMEM((nb, C, 256), BF16),
        pltpu.VMEM((nb, C, 256), BF16),
        pltpu.VMEM((nb, C, 256), BF16),
        pltpu.VMEM((nb, C, 256), BF16),
        pltpu.VMEM((nb, C, 256), BF16),
        pltpu.VMEM((27 * C, 128), F32),
        pltpu.VMEM((nd, 16, 256), F32),
        pltpu.VMEM((nd, 16, 256), F32),
        pltpu.VMEM((nb, 16, 256), BF16),
        pltpu.VMEM((nd, 16, 256), F32),
        pltpu.SemaphoreType.DMA((16,)),
        pltpu.SemaphoreType.DMA((16,)),
        pltpu.SemaphoreType.DMA((6, nb)),
        pltpu.SemaphoreType.DMA((6, nb)),
        pltpu.SemaphoreType.DMA((2, nd)),
        pltpu.SemaphoreType.DMA((2, nd)),
    ]
    results = pl.pallas_call(
        functools.partial(kernel, nd, nb),
        out_shape=(
            pltpu.VMEM((256, 256), BF16),
            pltpu.VMEM((8, 512, 128), F32),
            pltpu.VMEM((C, 27 * C), F32),
        ),
        in_specs=[hbm] * 10,
        out_specs=(vmem, vmem, vmem),
        scratch_shapes=scratch,
        compiler_params=pltpu.CompilerParams(
            collective_id=0, has_side_effects=True, vmem_limit_bytes=48 << 20
        ),
    )(*[pltpu.with_memory_space_constraint(one, pltpu.HBM) for one in inputs])
    fo, gf, gc = pl.pallas_call(
        store,
        out_shape=tuple(jax.ShapeDtypeStruct(one.shape, one.dtype) for one in results),
        in_specs=[vmem] * 3,
        out_specs=(hbm,) * 3,
        scratch_shapes=[pltpu.SemaphoreType.DMA((3,))],
        compiler_params=pltpu.CompilerParams(vmem_limit_bytes=1 << 20),
    )(*results)
    return fo, gf.reshape(8, C, 16, 128), gc


def solution(mesh):
    return jax.shard_map(
        functools.partial(body, mesh.shape["drift"], mesh.shape["beam"]),
        mesh=mesh,
        in_specs=(
            P("drift", None, "beam", None),
            P("drift", "beam", None),
            P("drift", "beam", None),
            P(),
            P(),
            P(),
            P(),
            P(("drift", "beam")),
            P(("drift", "beam")),
            P(("drift", "beam"), None),
        ),
        out_specs=(P(("drift", "beam"), None), P("drift", None, "beam", None), P()),
        check_vma=False,
    )
```

```python
import functools

import jax
import jax.numpy as jnp
from jax import lax
from jax.experimental import pallas as pl
from jax.experimental.pallas import tpu as pltpu
from jax.sharding import PartitionSpec as P

F32 = jnp.float32
BF16 = jnp.bfloat16
MESH = pl.DeviceIdType.MESH
C = 32
YB = 4
WIN = (YB + 2) * 3 * C
KC = 3 * WIN
NEAR = 11
NN = (((1,), (0,)), ((), ()))
NT = (((1,), (1,)), ((), ()))
TN = (((0,), (0,)), ((), ()))


def mm(lhs, rhs, dims):
    return lax.dot_general(lhs, rhs, dims, preferred_element_type=F32)


def sig_parts(value):
    sig = 1.0 / (1.0 + jnp.exp(-value))
    return value * sig, sig * (1.0 + value * (1.0 - sig))


def spread(cols, x, row, tile, lane):
    left = jnp.where(lane == 0, 0.0, pltpu.roll(tile, 1, 1)).astype(BF16)
    right = jnp.where(lane == 127, 0.0, pltpu.roll(tile, 127, 1)).astype(BF16)
    mid = tile.astype(BF16)
    for half in range(2):
        for k in range(2):
            inner = row - 8 * half - 4 * k
            if 0 <= inner < YB + 2:
                for tap, part in enumerate((left, mid, right)):
                    start = pl.multiple_of(x * WIN + inner * 96 + tap * C, C)
                    at = k * 256 + half * 128
                    cols[pl.ds(start, C), at : at + 128] = part


def widen(wide, weight):
    wide[...] = jnp.zeros_like(wide)
    for yo in range(YB):
        for a in range(3):
            at = a * WIN + yo * 96
            wide[yo * C : yo * C + C, at : at + 288] = weight[:, a * 288 : a * 288 + 288].astype(BF16)


def kernel(
    nd,
    nb,
    feat_in,
    occ_in,
    vf_in,
    cw_in,
    emb_in,
    mw_in,
    uw_in,
    es_in,
    et_in,
    cot_in,
    fo,
    gf,
    gc,
    feat,
    occ,
    vf,
    cw,
    emb,
    mw,
    uw,
    es,
    et,
    cot,
    in_sem,
    stage,
    flip,
    plain,
    cols,
    gcols,
    wide,
    gwide,
    lohot,
    lotall,
    hids,
    ahot,
    ahot1,
    slopes,
    bh,
    bc,
    bc1,
    res,
    sums,
    gbig,
    hx,
    hy,
    hc,
    gx,
    gy,
    gcn,
    cs,
    cr,
    ms,
    mr,
    pa,
    ms2,
    mr2,
    bm,
    gs,
    g1,
    g2s,
    g2,
    g3,
    hs,
    hr,
    ks,
    kr,
    ps,
    pr,
):
    d = lax.axis_index("drift")
    b = lax.axis_index("beam")
    dn, dp = lax.rem(d + 1, nd), lax.rem(d + nd - 1, nd)
    bn, bp = lax.rem(b + 1, nb), lax.rem(b + nb - 1, nb)

    loads = [
        pltpu.make_async_copy(src, dst, in_sem.at[i])
        for i, (src, dst) in enumerate(
            (
                (occ_in, occ),
                (feat_in, feat),
                (cw_in, cw),
                (vf_in, vf),
                (emb_in, emb),
                (mw_in, mw),
                (uw_in, uw),
                (es_in, es),
                (et_in, et),
                (cot_in, cot),
            )
        )
    ]
    barrier = pltpu.get_barrier_semaphore()

    def greet(dev):
        pl.semaphore_signal(barrier, inc=1, device_id=dev, device_id_type=MESH)

    def greet_beam(off, carry):
        greet((d, lax.rem(b + off, nb)))
        return carry

    def greet_drift(off, carry):
        greet((lax.rem(d + off, nd), b))
        return carry

    lax.fori_loop(1, nb, greet_beam, 0)
    lax.fori_loop(1, nd, greet_drift, 0)
    for dev in ((dn, bn), (dn, bp), (dp, bn), (dp, bp)):
        greet(dev)
    for copy in loads:
        copy.start()
    for copy in loads:
        copy.wait()

    lane = lax.broadcasted_iota(jnp.int32, (C, 128), 1)
    square = (C, C)
    eye = (
        lax.broadcasted_iota(jnp.int32, square, 0) == lax.broadcasted_iota(jnp.int32, square, 1)
    ).astype(F32).astype(BF16)
    group = lax.broadcasted_iota(jnp.int32, (1, 128), 1) // 8
    occ_f = occ[...].astype(F32)
    rows = []
    for j in range(2):
        row = jnp.zeros((1, 128), F32)
        for q in range(16):
            row = jnp.where(group == q, occ_f[j : j + 1, q : q + 1], row)
        rows.append(row)
    mrow = jnp.concatenate(rows, axis=1)
    x_lo = jnp.where(d > 0, 1.0, 0.0).astype(F32)
    x_hi = jnp.where(d < nd - 1, 1.0, 0.0).astype(F32)
    y_lo = jnp.where(b > 0, 1.0, 0.0).astype(F32)
    y_hi = jnp.where(b < nb - 1, 1.0, 0.0).astype(F32)

    def halo_copies(src, tx, ty, tc, base):
        plan = (
            (src.at[7, 480:512, :], tc.at[0], (dn, bn)),
            (src.at[7, 0:32, :], tc.at[1], (dn, bp)),
            (src.at[0, 480:512, :], tc.at[2], (dp, bn)),
            (src.at[0, 0:32, :], tc.at[3], (dp, bp)),
            (src.at[:, 480:512, :], ty.at[0], (d, bn)),
            (src.at[:, 0:32, :], ty.at[1], (d, bp)),
            (src.at[7], tx.at[0], (dn, b)),
            (src.at[0], tx.at[1], (dp, b)),
        )
        return [
            pltpu.make_async_remote_copy(
                src_ref=s,
                dst_ref=t,
                send_sem=hs.at[base + i],
                recv_sem=hr.at[base + i],
                device_id=dev,
                device_id_type=MESH,
            )
            for i, (s, t, dev) in enumerate(plan)
        ]

    def place_halos(target, tx, ty, tc):
        for y in range(16):
            spread(target, 0, y + 1, tx[0, y * C : y * C + C, :].astype(F32) * x_lo, lane)
            spread(target, 9, y + 1, tx[1, y * C : y * C + C, :].astype(F32) * x_hi, lane)

        def per_x(x, carry):
            spread(target, x + 1, 0, ty[0, x].astype(F32) * y_lo, lane)
            spread(target, x + 1, 17, ty[1, x].astype(F32) * y_hi, lane)
            return carry

        lax.fori_loop(0, 8, per_x, 0)
        spread(target, 0, 0, tc[0].astype(F32) * (x_lo * y_lo), lane)
        spread(target, 0, 17, tc[1].astype(F32) * (x_lo * y_hi), lane)
        spread(target, 9, 0, tc[2].astype(F32) * (x_hi * y_lo), lane)
        spread(target, 9, 17, tc[3].astype(F32) * (x_hi * y_hi), lane)

    by, bz = lax.rem(b, 4), b // 4
    near = sorted(range(16), key=lambda o: min(o % 4, 4 - o % 4) + min(o // 4, 4 - o // 4))
    far = near[:0:-1]

    def beam_copy(src, dst, base):
        def make(off):
            peer = 4 * lax.rem(bz + off // 4, 4) + lax.rem(by + off % 4, 4)
            return pltpu.make_async_remote_copy(
                src_ref=src(peer, off),
                dst_ref=dst(off) if callable(dst) else dst,
                send_sem=ks.at[base, off],
                recv_sem=kr.at[base, off],
                device_id=(d, peer),
                device_id_type=MESH,
            )

        return make

    def drift_copy(src, dst, base):
        def make(off):
            peer = lax.rem(d + off, nd)
            return pltpu.make_async_remote_copy(
                src_ref=src(peer),
                dst_ref=dst,
                send_sem=ps.at[base, off],
                recv_sem=pr.at[base, off],
                device_id=(peer, b),
                device_id_type=MESH,
            )

        return make

    def start_all(make, count):
        for off in far if count == nb else range(1, count):
            make(off).start()

    def wait_all(make, count):
        for off in range(1, count):
            make(off).wait()

    def load_row(x, carry):
        stage[...] = feat[x].astype(F32)
        for y in range(16):
            h = y // 8
            tile = stage[pl.ds(y, C, stride=16), :] * mrow[:, h * 128 : h * 128 + 128]
            plain[0, x, y * C : y * C + C, :] = tile.astype(BF16)
            spread(cols, x + 1, y + 1, tile, lane)
        return carry

    lax.fori_loop(0, 8, load_row, 0)
    pl.semaphore_wait(barrier, nb - 1 + nd - 1 + 4)
    halos = halo_copies(plain.at[0], hx, hy, hc, 0)
    for copy in halos:
        copy.start()

    sub_hi = lax.broadcasted_iota(jnp.int32, (16, 256), 0)
    sub_b = sub_hi.astype(F32).astype(BF16)
    one_b = jnp.ones((16, 256), BF16)
    zero_b = jnp.zeros((16, 256), BF16)
    lane_b = lax.broadcasted_iota(jnp.int32, (256, 128), 1).astype(F32).astype(BF16)
    one_c = jnp.ones((256, 128), BF16)
    zero_c = jnp.zeros((256, 128), BF16)

    def fids(x):
        return jnp.concatenate([vf[x, 0:8, :], vf[x, 8:16, :]], axis=1)

    def shift_of(x, sign):
        hi = fids(x) >> 8
        return ((((hi >> 2) - bz) * sign & 3) << 2) + (((hi & 3) - by) * sign & 3)

    def counts_of(x, total):
        ids = fids(x)
        columns = (ids & 255).astype(F32).T
        for k in range(2):
            parts = []
            for yo in range(YB):
                r = k * YB + yo
                one = ids[r : r + 1, :]
                lo = one & 255
                hi = one >> 8
                lo_b = jnp.broadcast_to(lo, (16, 256)).astype(F32).astype(BF16)
                for j in range(16):
                    lohot[2 * x + k, j * 16 : j * 16 + 16, yo * 256 : yo * 256 + 256] = jnp.where(
                        sub_b == lo_b - BF16(16 * j), one_b, zero_b
                    )
                col = jnp.broadcast_to(columns[:, r : r + 1], (256, 128)).astype(BF16)
                for j in range(2):
                    lotall[2 * x + k, yo * 256 : yo * 256 + 256, j * 128 : j * 128 + 128] = jnp.where(
                        col == lane_b + BF16(128 * j), one_c, zero_c
                    )
                parts.append(jnp.where(sub_hi == hi, mrow, 0.0).astype(BF16))
            total = total + mm(jnp.concatenate(parts, axis=1), lotall[2 * x + k], NN)
        return total

    counts = lax.fori_loop(0, 8, counts_of, jnp.zeros((16, 256), F32))
    for j in range(16):
        cs[j] = jnp.broadcast_to(counts[j : j + 1, :], (8, 256))
    cr[b] = cs[b]
    count_copies = beam_copy(lambda peer, off: cs.at[peer], cr.at[b], 0)
    start_all(count_copies, nb)

    widen(wide, cw)
    turned = mm(cw[...], eye, TN)
    for t in range(27):
        flip[:, (26 - t) * C : (27 - t) * C] = turned[t * C : t * C + C, :]
    widen(gwide, flip)
    for copy in halos:
        copy.wait()
    place_halos(cols, hx, hy, hc)

    sums[...] = jnp.zeros_like(sums)

    zero_h = jnp.zeros((C, 256), BF16)

    def fill(hot, r, shifts, hid, first, last):
        yo = r % YB
        row = jnp.broadcast_to(shifts[r : r + 1, :], (C, 256)).astype(F32).astype(BF16)
        for p in range(first, last):
            hot[p * C : p * C + C, yo * 256 : yo * 256 + 256] = jnp.where(
                row == BF16(near[p]), hid, zero_h
            )

    def convolve(x, k, hot):
        shifts = shift_of(x, 1)
        start = pl.multiple_of(x * WIN, C)
        conv = mm(wide[...], cols[pl.ds(start, KC), k * 256 : k * 256 + 256], NN)
        slopes[2 * x + k] = conv
        silu = conv / (1.0 + jnp.exp(-conv))
        for yo in range(YB):
            at = pl.multiple_of((x + 1) * WIN + (yo + 1) * 96 + C, C)
            act = cols[pl.ds(at, C), k * 256 : k * 256 + 256].astype(F32)
            hid = (mrow * (act + silu[yo * C : yo * C + C, :])).astype(BF16)
            hids[2 * x + k, yo * C : yo * C + C, :] = hid
            fill(hot, k * YB + yo, shifts, hid, NEAR, 16)

    def refill(x, k, hot):
        shifts = shift_of(x, 1)
        for yo in range(YB):
            fill(hot, k * YB + yo, shifts, hids[2 * x + k, yo * C : yo * C + C, :], 0, NEAR)

    def scatter_far(g, hot):
        sums[NEAR * C : 512, :] += mm(hot[NEAR * C : 512, :], lotall[g], NN)

    def scatter_near(g, hot):
        sums[0 : NEAR * C, :] += mm(hot[0 : NEAR * C, :], lotall[g], NN)

    def two_stage(make, use):
        def step(x, carry):
            use(2 * x, ahot)
            make(x, 1, ahot1)
            use(2 * x + 1, ahot1)
            make(x + 1, 0, ahot)
            return carry

        make(0, 0, ahot)
        lax.fori_loop(0, 7, step, 0)
        use(14, ahot)
        make(7, 1, ahot1)
        use(15, ahot1)

    sum_copies = beam_copy(
        lambda peer, off: ms.at[near.index(off)], lambda off: mr.at[near.index(off)], 1
    )
    two_stage(convolve, scatter_far)
    for p in range(15, NEAR - 1, -1):
        ms[p] = sums[p * C : p * C + C, :].astype(BF16)
        sum_copies(near[p]).start()
    two_stage(refill, scatter_near)
    for p in range(NEAR - 1, 0, -1):
        ms[p] = sums[p * C : p * C + C, :].astype(BF16)
        sum_copies(near[p]).start()
    mr[0] = sums[0:C, :].astype(BF16)

    def slope_of(g, carry):
        sig = 1.0 / (1.0 + jnp.exp(-slopes[g]))
        slopes[g] = mrow * (sig * (1.0 + slopes[g] * (1.0 - sig)))
        return carry

    lax.fori_loop(0, 16, slope_of, 0)

    sub_e = lax.broadcasted_iota(jnp.int32, (256, 1024), 0)
    src = es[...]
    src_lo = (sub_e == (src & 255)).astype(F32).astype(BF16)
    src_hi = src >> 8
    dst_hot = (sub_e == et[...]).astype(F32).astype(BF16)
    back_agg = mm(cot[...], uw[...], NT).astype(BF16)
    agg_edge = mm(back_agg, dst_hot, TN)

    wait_all(count_copies, nb)
    wait_all(sum_copies, nb)
    total = mr[0].astype(F32)
    number = cr[0]
    for j in range(1, 16):
        total = total + mr[j].astype(F32)
        number = number + cr[j]
    inverse = 1.0 / jnp.maximum(number[0:1, :], 1.0)
    pooled = (total * inverse).astype(BF16)
    pa[b] = pooled
    pool_copies = beam_copy(lambda peer, off: pa.at[b], pa.at[b], 2)
    start_all(pool_copies, nb)

    pre_own = mm(pooled, emb[...], TN)
    silu_own, slope_own = sig_parts(pre_own)
    own = silu_own.astype(BF16)
    back_self = mm(emb[...], (cot[...].astype(F32) * slope_own).astype(BF16), NT)

    wait_all(pool_copies, nb)
    table = pa[...].reshape(16 * C, 256)
    picked = jnp.zeros((C, 1024), F32)
    every = mm(table, src_lo, NN)
    for q in range(16):
        picked = jnp.where(src_hi == q, every[q * C : q * C + C, :], picked)
    pre_src = mm(emb[...], picked.astype(BF16), TN)
    silu_src, slope_src = sig_parts(pre_src)
    pre_msg = mm(mw[...], silu_src.astype(BF16), TN)
    silu_msg, slope_msg = sig_parts(pre_msg)
    back_pre = (agg_edge * slope_msg).astype(BF16)
    back_src = mm(mw[...], back_pre, NN)
    back_edge = mm(emb[...], (back_src * slope_src).astype(BF16), NN)
    for q in range(16):
        ahot[q * C : q * C + C, :] = jnp.where(src_hi == q, back_edge, 0.0).astype(BF16)
    back_sums = mm(ahot[...], src_lo, NT)
    for j in range(16):
        ms2[j] = back_sums[j * C : j * C + C, :].astype(BF16)
    mr2[b] = ms2[b]
    back_copies = beam_copy(lambda peer, off: ms2.at[peer], mr2.at[b], 3)
    start_all(back_copies, nb)

    gathered = mm(dst_hot, silu_msg.astype(BF16), NT).astype(BF16)
    fo[...] = (own.astype(F32) + mm(gathered, uw[...], NN)).astype(BF16)

    wait_all(back_copies, nb)
    remote = back_self
    for j in range(16):
        remote = remote + mr2[j].astype(F32)
    bm[0] = (remote * inverse).astype(BF16)
    mean_copies = beam_copy(lambda peer, off: bm.at[0], lambda off: bm.at[near.index(off)], 4)
    start_all(mean_copies, nb)
    gbig[...] = jnp.zeros_like(gbig)
    for off in near[1:NEAR]:
        mean_copies(off).wait()

    def gather_near(x, carry):
        shifts = shift_of(x, -1)
        means = bm[0:NEAR].reshape(NEAR * C, 256)
        for k in range(2):
            for yo in range(YB):
                r = k * YB + yo
                hi = shifts[r : r + 1, :]
                res[0 : NEAR * C, :] = mm(means, lohot[2 * x + k, :, yo * 256 : yo * 256 + 256], NN)
                hid = res[0:C, :]
                for q in range(1, NEAR):
                    hid = jnp.where(hi == near[q], res[q * C : q * C + C, :], hid)
                bh[2 * x + k, yo * C : yo * C + C, :] = hid.astype(BF16)
        return carry

    lax.fori_loop(0, 8, gather_near, 0)
    for off in near[NEAR:]:
        mean_copies(off).wait()

    def gather_far(i, out):
        means = bm[NEAR:16].reshape((16 - NEAR) * C, 256)
        for j in range(2):
            x = 2 * i + j
            shifts = shift_of(x, -1)
            for k in range(2):
                g = 2 * x + k
                for yo in range(YB):
                    r = k * YB + yo
                    hi = shifts[r : r + 1, :]
                    got = mm(means, lohot[g, :, yo * 256 : yo * 256 + 256], NN)
                    hid = bh[g, yo * C : yo * C + C, :].astype(F32)
                    for q in range(NEAR, 16):
                        at = (q - NEAR) * C
                        hid = jnp.where(hi == near[q], got[at : at + C, :], hid)
                    bh[g, yo * C : yo * C + C, :] = hid.astype(BF16)
                    back = hid * slopes[g, yo * C : yo * C + C, :]
                    row = j * YB * C + yo * C
                    out[row : row + C, k * 256 : k * 256 + 256] = back.astype(BF16)
                    for h in range(2):
                        y = 8 * h + YB * k + yo
                        tile = back[:, h * 128 : h * 128 + 128]
                        plain[1, x, y * C : y * C + C, :] = tile.astype(BF16)
                        spread(gcols, x + 1, y + 1, tile, lane)

    def weights(i, back):
        start = pl.multiple_of(2 * i * WIN, C)
        gbig[...] += mm(cols[pl.ds(start, 4 * WIN), :], back[...], NT)

    def backward(i, carry):
        weights(i, bc)
        gather_far(i + 1, bc1)
        bc[...] = bc1[...]
        return carry

    gather_far(0, bc)
    lax.fori_loop(0, 3, backward, 0)
    back_halos = halo_copies(plain.at[1], gx, gy, gcn, 8)
    for copy in back_halos:
        copy.start()
    weights(3, bc)
    quarter = lax.broadcasted_iota(jnp.int32, (288, 128), 1) // C
    for a in range(3):
        total = None
        for j in range(2):
            at = (j + a) * WIN
            part = gbig[at : at + 288, j * 128 : j * 128 + 128]
            for yo in range(1, YB):
                down = at + yo * 96
                part = jnp.where(
                    quarter == yo, gbig[down : down + 288, j * 128 : j * 128 + 128], part
                )
            total = part if total is None else total + part
        total = total + pltpu.roll(total, 64, 1)
        gs[a * 288 : a * 288 + 288, :] = total + pltpu.roll(total, 32, 1)
    packed = gs[0:216, :]
    for j in range(1, 4):
        packed = jnp.where(quarter[0:216] == j, gs[j * 216 : j * 216 + 216, :], packed)
    turned = jnp.concatenate([packed, jnp.zeros((40, 128), F32)], axis=0).T
    for j in range(8):
        g2s[j] = turned[j * 16 : j * 16 + 16, :]
    g1[d] = g2s[d]
    first = drift_copy(lambda peer: g2s.at[peer], g1.at[d], 0)
    start_all(first, nd)

    def conv_back(x, carry):
        for k in range(2):
            g = 2 * x + k
            start = pl.multiple_of(x * WIN, C)
            conv = mm(gwide[...], gcols[pl.ds(start, KC), k * 256 : k * 256 + 256], NN)
            full = mrow * (conv + bh[g].astype(F32))
            for yo in range(YB):
                for h in range(2):
                    y = 8 * h + YB * k + yo
                    gf[x, pl.ds(y, C, stride=16), :] = full[
                        yo * C : yo * C + C, h * 128 : h * 128 + 128
                    ]
        return carry

    wait_all(first, nd)
    part = g1[0]
    for j in range(1, 8):
        part = part + g1[j]
    g2[b] = part.astype(BF16)
    second = beam_copy(lambda peer, off: g2.at[b], g2.at[b], 5)
    start_all(second, nb)
    for copy in back_halos:
        copy.wait()
    place_halos(gcols, gx, gy, gcn)
    lax.fori_loop(0, 3, conv_back, 0)
    wait_all(second, nb)
    part = g2[0].astype(F32)
    for j in range(1, 16):
        part = part + g2[j].astype(F32)
    g3[d] = part
    third = drift_copy(lambda peer: g3.at[d], g3.at[d], 1)
    start_all(third, nd)
    lax.fori_loop(3, 8, conv_back, 0)
    wait_all(third, nd)
    for j in range(8):
        at = (j // 2) * 216
        gc[(j % 2) * 16 : (j % 2) * 16 + 16, at : at + 216] = g3[j, :, 0:216]


def store(fo, gf, gc, fo_out, gf_out, gc_out, sem):
    copies = [
        pltpu.make_async_copy(src, dst, sem.at[i])
        for i, (src, dst) in enumerate(((gf, gf_out), (fo, fo_out), (gc, gc_out)))
    ]
    for copy in copies:
        copy.start()
    for copy in copies:
        copy.wait()


def body(nd, nb, features, occupied, fragments, cw, emb, mw, uw, es, et, cot):
    vmem = pl.BlockSpec(memory_space=pltpu.VMEM)
    hbm = pl.BlockSpec(memory_space=pltpu.HBM)
    inputs = (
        features.reshape(8, 512, 128),
        occupied.reshape(2, 16),
        fragments,
        cw,
        emb,
        mw,
        uw,
        es.reshape(1, -1),
        et.reshape(1, -1),
        cot,
    )
    scratch = [pltpu.VMEM(one.shape, one.dtype) for one in inputs] + [
        pltpu.SemaphoreType.DMA((10,)),
        pltpu.VMEM((512, 128), F32),
        pltpu.VMEM((C, 27 * C), F32),
        pltpu.VMEM((2, 8, 512, 128), BF16),
        pltpu.VMEM((10 * WIN, 512), BF16),
        pltpu.VMEM((10 * WIN, 512), BF16),
        pltpu.VMEM((YB * C, KC), BF16),
        pltpu.VMEM((YB * C, KC), BF16),
        pltpu.VMEM((16, 256, 1024), BF16),
        pltpu.VMEM((16, 1024, 256), BF16),
        pltpu.VMEM((16, YB * C, 256), BF16),
        pltpu.VMEM((512, 1024), BF16),
        pltpu.VMEM((512, 1024), BF16),
        pltpu.VMEM((16, YB * C, 256), F32),
        pltpu.VMEM((16, YB * C, 256), BF16),
        pltpu.VMEM((2 * YB * C, 512), BF16),
        pltpu.VMEM((2 * YB * C, 512), BF16),
        pltpu.VMEM((512, 256), F32),
        pltpu.VMEM((512, 256), F32),
        pltpu.VMEM((4 * WIN, 256), F32),
        pltpu.VMEM((2, 512, 128), BF16),
        pltpu.VMEM((2, 8, C, 128), BF16),
        pltpu.VMEM((4, C, 128), BF16),
        pltpu.VMEM((2, 512, 128), BF16),
        pltpu.VMEM((2, 8, C, 128), BF16),
        pltpu.VMEM((4, C, 128), BF16),
        pltpu.VMEM((nb, 8, 256), F32),
        pltpu.VMEM((nb, 8, 256), F32),
        pltpu.VMEM((nb, C, 256), BF16),
        pltpu.VMEM((nb, C, 256), BF16),
        pltpu.VMEM((nb, C, 256), BF16),
        pltpu.VMEM((nb, C, 256), BF16),
        pltpu.VMEM((nb, C, 256), BF16),
        pltpu.VMEM((nb, C, 256), BF16),
        pltpu.VMEM((27 * C, 128), F32),
        pltpu.VMEM((nd, 16, 256), F32),
        pltpu.VMEM((nd, 16, 256), F32),
        pltpu.VMEM((nb, 16, 256), BF16),
        pltpu.VMEM((nd, 16, 256), F32),
        pltpu.SemaphoreType.DMA((16,)),
        pltpu.SemaphoreType.DMA((16,)),
        pltpu.SemaphoreType.DMA((6, nb)),
        pltpu.SemaphoreType.DMA((6, nb)),
        pltpu.SemaphoreType.DMA((2, nd)),
        pltpu.SemaphoreType.DMA((2, nd)),
    ]
    results = pl.pallas_call(
        functools.partial(kernel, nd, nb),
        out_shape=(
            pltpu.VMEM((256, 256), BF16),
            pltpu.VMEM((8, 512, 128), F32),
            pltpu.VMEM((C, 27 * C), F32),
        ),
        in_specs=[hbm] * 10,
        out_specs=(vmem, vmem, vmem),
        scratch_shapes=scratch,
        compiler_params=pltpu.CompilerParams(
            collective_id=0, has_side_effects=True, vmem_limit_bytes=57 << 20
        ),
    )(*[pltpu.with_memory_space_constraint(one, pltpu.HBM) for one in inputs])
    fo, gf, gc = pl.pallas_call(
        store,
        out_shape=tuple(jax.ShapeDtypeStruct(one.shape, one.dtype) for one in results),
        in_specs=[vmem] * 3,
        out_specs=(hbm,) * 3,
        scratch_shapes=[pltpu.SemaphoreType.DMA((3,))],
        compiler_params=pltpu.CompilerParams(vmem_limit_bytes=1 << 20),
    )(*results)
    return fo, gf.reshape(8, C, 16, 128), gc


def solution(mesh):
    return jax.shard_map(
        functools.partial(body, mesh.shape["drift"], mesh.shape["beam"]),
        mesh=mesh,
        in_specs=(
            P("drift", None, "beam", None),
            P("drift", "beam", None),
            P("drift", "beam", None),
            P(),
            P(),
            P(),
            P(),
            P(("drift", "beam")),
            P(("drift", "beam")),
            P(("drift", "beam"), None),
        ),
        out_specs=(P(("drift", "beam"), None), P("drift", None, "beam", None), P()),
        check_vma=False,
    )
```

```python
import functools

import jax
import jax.numpy as jnp
from jax import lax
from jax.experimental import pallas as pl
from jax.experimental.pallas import tpu as pltpu
from jax.sharding import PartitionSpec as P

F32 = jnp.float32
BF16 = jnp.bfloat16
MESH = pl.DeviceIdType.MESH
C = 32
YB = 4
WIN = (YB + 2) * 3 * C
KC = 3 * WIN
NEAR = 11
CLOSE = 5
EC = 1
NN = (((1,), (0,)), ((), ()))
NT = (((1,), (1,)), ((), ()))
TN = (((0,), (0,)), ((), ()))


def mm(lhs, rhs, dims):
    return lax.dot_general(lhs, rhs, dims, preferred_element_type=F32)


def sig_parts(value):
    sig = 1.0 / (1.0 + jnp.exp(-value))
    return value * sig, sig * (1.0 + value * (1.0 - sig))


def spread(cols, x, row, tile, lane):
    left = jnp.where(lane == 0, 0.0, pltpu.roll(tile, 1, 1)).astype(BF16)
    right = jnp.where(lane == 127, 0.0, pltpu.roll(tile, 127, 1)).astype(BF16)
    mid = tile.astype(BF16)
    for half in range(2):
        for k in range(2):
            inner = row - 8 * half - 4 * k
            if 0 <= inner < YB + 2:
                for tap, part in enumerate((left, mid, right)):
                    start = pl.multiple_of(x * WIN + inner * 96 + tap * C, C)
                    at = k * 256 + half * 128
                    cols[pl.ds(start, C), at : at + 128] = part


def widen(wide, weight):
    wide[...] = jnp.zeros_like(wide)
    for yo in range(YB):
        for a in range(3):
            at = a * WIN + yo * 96
            wide[yo * C : yo * C + C, at : at + 288] = weight[:, a * 288 : a * 288 + 288].astype(BF16)


def kernel(
    nd,
    nb,
    feat_in,
    occ_in,
    vf_in,
    cw_in,
    emb_in,
    mw_in,
    uw_in,
    es_in,
    et_in,
    cot_in,
    fo,
    gf,
    gc,
    feat,
    occ,
    vf,
    cw,
    emb,
    mw,
    uw,
    es,
    et,
    cot,
    in_sem,
    stage,
    flip,
    plain,
    cols,
    gcols,
    wide,
    gwide,
    lohot,
    lotall,
    hids,
    ahot,
    ahot1,
    slopes,
    bh,
    bc,
    bc1,
    sums,
    gbig,
    hx,
    hy,
    hc,
    gx,
    gy,
    gcn,
    cs,
    cr,
    ms,
    mr,
    pa,
    ms2,
    mr2,
    bm,
    gs,
    g1,
    g2s,
    g2,
    g3,
    hs,
    hr,
    ks,
    kr,
    ps,
    pr,
):
    d = lax.axis_index("drift")
    b = lax.axis_index("beam")
    dn, dp = lax.rem(d + 1, nd), lax.rem(d + nd - 1, nd)
    bn, bp = lax.rem(b + 1, nb), lax.rem(b + nb - 1, nb)

    loads = [
        pltpu.make_async_copy(src, dst, in_sem.at[i])
        for i, (src, dst) in enumerate(
            (
                (occ_in, occ),
                (feat_in, feat),
                (cw_in, cw),
                (vf_in, vf),
                (emb_in, emb),
                (mw_in, mw),
                (uw_in, uw),
                (es_in, es),
                (et_in, et),
                (cot_in, cot),
            )
        )
    ]
    barrier = pltpu.get_barrier_semaphore()

    def greet(dev):
        pl.semaphore_signal(barrier, inc=1, device_id=dev, device_id_type=MESH)

    def greet_beam(off, carry):
        greet((d, lax.rem(b + off, nb)))
        return carry

    def greet_drift(off, carry):
        greet((lax.rem(d + off, nd), b))
        return carry

    lax.fori_loop(1, nb, greet_beam, 0)
    lax.fori_loop(1, nd, greet_drift, 0)
    for dev in ((dn, bn), (dn, bp), (dp, bn), (dp, bp)):
        greet(dev)
    for copy in loads:
        copy.start()
    loads[0].wait()
    loads[1].wait()

    lane = lax.broadcasted_iota(jnp.int32, (C, 128), 1)
    square = (C, C)
    eye = (
        lax.broadcasted_iota(jnp.int32, square, 0) == lax.broadcasted_iota(jnp.int32, square, 1)
    ).astype(F32).astype(BF16)
    group = lax.broadcasted_iota(jnp.int32, (1, 128), 1) // 8
    occ_f = occ[...].astype(F32)
    rows = []
    for j in range(2):
        row = jnp.zeros((1, 128), F32)
        for q in range(16):
            row = jnp.where(group == q, occ_f[j : j + 1, q : q + 1], row)
        rows.append(row)
    mrow = jnp.concatenate(rows, axis=1)
    x_lo = jnp.where(d > 0, 1.0, 0.0).astype(F32)
    x_hi = jnp.where(d < nd - 1, 1.0, 0.0).astype(F32)
    y_lo = jnp.where(b > 0, 1.0, 0.0).astype(F32)
    y_hi = jnp.where(b < nb - 1, 1.0, 0.0).astype(F32)

    def halo_copies(src, tx, ty, tc, base):
        plan = (
            (src.at[7, 480:512, :], tc.at[0], (dn, bn)),
            (src.at[7, 0:32, :], tc.at[1], (dn, bp)),
            (src.at[0, 480:512, :], tc.at[2], (dp, bn)),
            (src.at[0, 0:32, :], tc.at[3], (dp, bp)),
            (src.at[:, 480:512, :], ty.at[0], (d, bn)),
            (src.at[:, 0:32, :], ty.at[1], (d, bp)),
            (src.at[7], tx.at[0], (dn, b)),
            (src.at[0], tx.at[1], (dp, b)),
        )
        return [
            pltpu.make_async_remote_copy(
                src_ref=s,
                dst_ref=t,
                send_sem=hs.at[base + i],
                recv_sem=hr.at[base + i],
                device_id=dev,
                device_id_type=MESH,
            )
            for i, (s, t, dev) in enumerate(plan)
        ]

    def place_halos(target, tx, ty, tc):
        for y in range(16):
            spread(target, 0, y + 1, tx[0, y * C : y * C + C, :].astype(F32) * x_lo, lane)
            spread(target, 9, y + 1, tx[1, y * C : y * C + C, :].astype(F32) * x_hi, lane)

        def per_x(x, carry):
            spread(target, x + 1, 0, ty[0, x].astype(F32) * y_lo, lane)
            spread(target, x + 1, 17, ty[1, x].astype(F32) * y_hi, lane)
            return carry

        lax.fori_loop(0, 8, per_x, 0)
        spread(target, 0, 0, tc[0].astype(F32) * (x_lo * y_lo), lane)
        spread(target, 0, 17, tc[1].astype(F32) * (x_lo * y_hi), lane)
        spread(target, 9, 0, tc[2].astype(F32) * (x_hi * y_lo), lane)
        spread(target, 9, 17, tc[3].astype(F32) * (x_hi * y_hi), lane)

    by, bz = lax.rem(b, 4), b // 4
    near = sorted(range(16), key=lambda o: min(o % 4, 4 - o % 4) + min(o // 4, 4 - o // 4))
    far = near[:0:-1]

    def beam_copy(src, dst, base):
        def make(off):
            peer = 4 * lax.rem(bz + off // 4, 4) + lax.rem(by + off % 4, 4)
            return pltpu.make_async_remote_copy(
                src_ref=src(peer, off),
                dst_ref=dst(off) if callable(dst) else dst,
                send_sem=ks.at[base, off],
                recv_sem=kr.at[base, off],
                device_id=(d, peer),
                device_id_type=MESH,
            )

        return make

    def drift_copy(src, dst, base):
        def make(off):
            peer = lax.rem(d + off, nd)
            return pltpu.make_async_remote_copy(
                src_ref=src(peer),
                dst_ref=dst,
                send_sem=ps.at[base, off],
                recv_sem=pr.at[base, off],
                device_id=(peer, b),
                device_id_type=MESH,
            )

        return make

    def start_all(make, count):
        for off in far if count == nb else range(1, count):
            make(off).start()

    def wait_all(make, count):
        for off in range(1, count):
            make(off).wait()

    def load_row(x, carry):
        stage[...] = feat[x].astype(F32)
        for y in range(16):
            h = y // 8
            tile = stage[pl.ds(y, C, stride=16), :] * mrow[:, h * 128 : h * 128 + 128]
            plain[0, x, y * C : y * C + C, :] = tile.astype(BF16)
            spread(cols, x + 1, y + 1, tile, lane)
        return carry

    lax.fori_loop(0, 8, load_row, 0)
    pl.semaphore_wait(barrier, nb - 1 + nd - 1 + 4)
    halos = halo_copies(plain.at[0], hx, hy, hc, 0)
    for copy in halos:
        copy.start()

    sub_hi = lax.broadcasted_iota(jnp.int32, (16, 256), 0)
    sub_b = sub_hi.astype(F32).astype(BF16)
    one_b = jnp.ones((16, 256), BF16)
    zero_b = jnp.zeros((16, 256), BF16)
    lane_b = lax.broadcasted_iota(jnp.int32, (256, 128), 1).astype(F32).astype(BF16)
    one_c = jnp.ones((256, 128), BF16)
    zero_c = jnp.zeros((256, 128), BF16)

    def fids(x):
        return jnp.concatenate([vf[x, 0:8, :], vf[x, 8:16, :]], axis=1)

    def shift_of(x, sign):
        hi = fids(x) >> 8
        return ((((hi >> 2) - bz) * sign & 3) << 2) + (((hi & 3) - by) * sign & 3)

    def one_hots(x, carry):
        ids = fids(x) & 255
        columns = ids.astype(F32).T
        for k in range(2):
            for yo in range(YB):
                r = k * YB + yo
                col = jnp.broadcast_to(columns[:, r : r + 1], (256, 128)).astype(BF16)
                for j in range(2):
                    lotall[2 * x + k, yo * 256 : yo * 256 + 256, j * 128 : j * 128 + 128] = jnp.where(
                        col == lane_b + BF16(128 * j), one_c, zero_c
                    )
                lo_b = jnp.broadcast_to(ids[r : r + 1, :], (16, 256)).astype(F32).astype(BF16)
                for j in range(16):
                    lohot[2 * x + k, j * 16 : j * 16 + 16, yo * 256 : yo * 256 + 256] = jnp.where(
                        sub_b == lo_b - BF16(16 * j), one_b, zero_b
                    )
        return carry

    loads[3].wait()
    lax.fori_loop(0, 8, one_hots, 0)

    loads[2].wait()
    widen(wide, cw)
    turned = mm(cw[...], eye, TN)
    for t in range(27):
        flip[:, (26 - t) * C : (27 - t) * C] = turned[t * C : t * C + C, :]
    widen(gwide, flip)
    for copy in halos:
        copy.wait()
    place_halos(cols, hx, hy, hc)

    sums[...] = jnp.zeros_like(sums)

    zero_h = jnp.zeros((C, 256), BF16)

    def fill(hot, r, shifts, hid, first, last):
        yo = r % YB
        row = jnp.broadcast_to(shifts[r : r + 1, :], (C, 256)).astype(F32).astype(BF16)
        for p in range(first, last):
            hot[p * C : p * C + C, yo * 256 : yo * 256 + 256] = jnp.where(
                row == BF16(near[p]), hid, zero_h
            )

    def convolve(x, k, hot):
        shifts = shift_of(x, 1)
        owners = fids(x) >> 8
        start = pl.multiple_of(x * WIN, C)
        conv = mm(wide[...], cols[pl.ds(start, KC), k * 256 : k * 256 + 256], NN)
        slopes[2 * x + k] = conv
        silu = conv / (1.0 + jnp.exp(-conv))
        for yo in range(YB):
            at = pl.multiple_of((x + 1) * WIN + (yo + 1) * 96 + C, C)
            act = cols[pl.ds(at, C), k * 256 : k * 256 + 256].astype(F32)
            hid = (mrow * (act + silu[yo * C : yo * C + C, :])).astype(BF16)
            hids[2 * x + k, yo * C : yo * C + C, :] = hid
            r = k * YB + yo
            fill(hot, r, shifts, hid, NEAR, 16)
            hot[512:528, yo * 256 : yo * 256 + 256] = jnp.where(
                sub_hi == owners[r : r + 1, :], mrow, 0.0
            ).astype(BF16)

    def refill(x, k, hot):
        shifts = shift_of(x, 1)
        for yo in range(YB):
            fill(hot, k * YB + yo, shifts, hids[2 * x + k, yo * C : yo * C + C, :], 0, NEAR)

    def scatter_far(g, hot):
        sums[NEAR * C : 528, :] += mm(hot[NEAR * C : 528, :], lotall[g], NN)

    def scatter_near(g, hot):
        sums[0 : NEAR * C, :] += mm(hot[0 : NEAR * C, :], lotall[g], NN)

    def two_stage(make, use):
        def step(x, carry):
            use(2 * x, ahot)
            make(x, 1, ahot1)
            use(2 * x + 1, ahot1)
            make(x + 1, 0, ahot)
            return carry

        make(0, 0, ahot)
        lax.fori_loop(0, 7, step, 0)
        use(14, ahot)
        make(7, 1, ahot1)
        use(15, ahot1)

    sum_copies = beam_copy(
        lambda peer, off: ms.at[near.index(off)], lambda off: mr.at[near.index(off)], 1
    )
    two_stage(convolve, scatter_far)
    for p in range(15, NEAR - 1, -1):
        ms[p] = sums[p * C : p * C + C, :].astype(BF16)
        sum_copies(near[p]).start()
    for j in range(16):
        cs[j] = jnp.broadcast_to(sums[512 + j : 513 + j, :], (8, 256))
    cr[b] = cs[b]
    count_copies = beam_copy(lambda peer, off: cs.at[peer], cr.at[b], 0)
    start_all(count_copies, nb)
    two_stage(refill, scatter_near)
    for p in range(NEAR - 1, 0, -1):
        ms[p] = sums[p * C : p * C + C, :].astype(BF16)
        sum_copies(near[p]).start()
    mr[0] = sums[0:C, :].astype(BF16)

    def slope_of(g, carry):
        sig = 1.0 / (1.0 + jnp.exp(-slopes[g]))
        slopes[g] = mrow * (sig * (1.0 + slopes[g] * (1.0 - sig)))
        return carry

    lax.fori_loop(0, 16, slope_of, 0)

    for i in range(4, 10):
        loads[i].wait()
    sub_e = lax.broadcasted_iota(jnp.int32, (256, 1024), 0)
    src = es[...]
    src_lo = (sub_e == (src & 255)).astype(F32).astype(BF16)
    src_hi = src >> 8
    dst_hot = (sub_e == et[...]).astype(F32).astype(BF16)
    back_agg = mm(cot[...], uw[...], NT).astype(BF16)
    agg_edge = mm(back_agg, dst_hot, TN)

    wait_all(count_copies, nb)
    wait_all(sum_copies, nb)
    total = mr[0].astype(F32)
    number = cr[0]
    for j in range(1, 16):
        total = total + mr[j].astype(F32)
        number = number + cr[j]
    inverse = 1.0 / jnp.maximum(number[0:1, :], 1.0)
    pooled = (total * inverse).astype(BF16)
    pa[b] = pooled
    pool_copies = beam_copy(lambda peer, off: pa.at[b], pa.at[b], 2)
    start_all(pool_copies, nb)

    pre_own = mm(pooled, emb[...], TN)
    silu_own, slope_own = sig_parts(pre_own)
    own = silu_own.astype(BF16)
    back_self = mm(emb[...], (cot[...].astype(F32) * slope_own).astype(BF16), NT)

    wait_all(pool_copies, nb)
    table = pa[...].reshape(16 * C, 256)
    msgs = []
    for e in range(EC):
        w = 1024 // EC
        cut = slice(e * w, e * w + w)
        every = mm(table, src_lo[:, cut], NN)
        picked = every[0:C, :]
        for q in range(1, 16):
            picked = jnp.where(src_hi[:, cut] == q, every[q * C : q * C + C, :], picked)
        pre_src = mm(emb[...], picked.astype(BF16), TN)
        silu_src, slope_src = sig_parts(pre_src)
        pre_msg = mm(mw[...], silu_src.astype(BF16), TN)
        silu_msg, slope_msg = sig_parts(pre_msg)
        msgs.append(silu_msg.astype(BF16))
        back_pre = (agg_edge[:, cut] * slope_msg).astype(BF16)
        back_src = mm(mw[...], back_pre, NN)
        back_edge = mm(emb[...], (back_src * slope_src).astype(BF16), NN)
        for q in range(16):
            ahot[q * C : q * C + C, cut] = jnp.where(src_hi[:, cut] == q, back_edge, 0.0).astype(
                BF16
            )
    back_sums = mm(ahot[0:512, :], src_lo, NT)
    for j in range(16):
        ms2[j] = back_sums[j * C : j * C + C, :].astype(BF16)
    mr2[b] = ms2[b]
    back_copies = beam_copy(lambda peer, off: ms2.at[peer], mr2.at[b], 3)
    start_all(back_copies, nb)

    gathered = mm(dst_hot, jnp.concatenate(msgs, axis=1), NT).astype(BF16)
    fo[...] = (own.astype(F32) + mm(gathered, uw[...], NN)).astype(BF16)

    wait_all(back_copies, nb)
    remote = back_self
    for j in range(16):
        remote = remote + mr2[j].astype(F32)
    bm[0] = (remote * inverse).astype(BF16)
    mean_copies = beam_copy(lambda peer, off: bm.at[0], lambda off: bm.at[near.index(off)], 4)
    for off in near[1:]:
        mean_copies(off).start()
    gbig[...] = jnp.zeros_like(gbig)
    for off in near[1:CLOSE]:
        mean_copies(off).wait()

    def gather_near(x, carry):
        shifts = shift_of(x, -1)
        means = bm[0:CLOSE].reshape(CLOSE * C, 256)
        for k in range(2):
            for yo in range(YB):
                r = k * YB + yo
                hi = shifts[r : r + 1, :]
                got = mm(means, lohot[2 * x + k, :, yo * 256 : yo * 256 + 256], NN)
                hid = got[0:C, :]
                for q in range(1, CLOSE):
                    hid = jnp.where(hi == near[q], got[q * C : q * C + C, :], hid)
                bh[2 * x + k, yo * C : yo * C + C, :] = hid.astype(BF16)
        return carry

    lax.fori_loop(0, 8, gather_near, 0)
    for off in near[CLOSE:]:
        mean_copies(off).wait()

    def gather_far(i, out):
        means = bm[CLOSE:16].reshape((16 - CLOSE) * C, 256)
        for j in range(2):
            x = 2 * i + j
            shifts = shift_of(x, -1)
            for k in range(2):
                g = 2 * x + k
                for yo in range(YB):
                    r = k * YB + yo
                    hi = shifts[r : r + 1, :]
                    got = mm(means, lohot[g, :, yo * 256 : yo * 256 + 256], NN)
                    hid = bh[g, yo * C : yo * C + C, :].astype(F32)
                    for q in range(CLOSE, 16):
                        at = (q - CLOSE) * C
                        hid = jnp.where(hi == near[q], got[at : at + C, :], hid)
                    bh[g, yo * C : yo * C + C, :] = hid.astype(BF16)
                    back = hid * slopes[g, yo * C : yo * C + C, :]
                    row = j * YB * C + yo * C
                    out[row : row + C, k * 256 : k * 256 + 256] = back.astype(BF16)
                    for h in range(2):
                        y = 8 * h + YB * k + yo
                        tile = back[:, h * 128 : h * 128 + 128]
                        plain[1, x, y * C : y * C + C, :] = tile.astype(BF16)
                        spread(gcols, x + 1, y + 1, tile, lane)

    def weights(i, back):
        start = pl.multiple_of(2 * i * WIN, C)
        gbig[...] += mm(cols[pl.ds(start, 4 * WIN), :], back[...], NT)

    def backward(i, carry):
        weights(i, bc)
        gather_far(i + 1, bc1)
        bc[...] = bc1[...]
        return carry

    gather_far(0, bc)
    lax.fori_loop(0, 3, backward, 0)
    back_halos = halo_copies(plain.at[1], gx, gy, gcn, 8)
    for copy in back_halos:
        copy.start()
    weights(3, bc)
    quarter = lax.broadcasted_iota(jnp.int32, (288, 128), 1) // C
    for a in range(3):
        total = None
        for j in range(2):
            at = (j + a) * WIN
            part = gbig[at : at + 288, j * 128 : j * 128 + 128]
            for yo in range(1, YB):
                down = at + yo * 96
                part = jnp.where(
                    quarter == yo, gbig[down : down + 288, j * 128 : j * 128 + 128], part
                )
            total = part if total is None else total + part
        total = total + pltpu.roll(total, 64, 1)
        gs[a * 288 : a * 288 + 288, :] = total + pltpu.roll(total, 32, 1)
    packed = gs[0:216, :]
    for j in range(1, 4):
        packed = jnp.where(quarter[0:216] == j, gs[j * 216 : j * 216 + 216, :], packed)
    turned = jnp.concatenate([packed, jnp.zeros((40, 128), F32)], axis=0).T
    for j in range(8):
        g2s[j] = turned[j * 16 : j * 16 + 16, :]
    g1[d] = g2s[d]
    first = drift_copy(lambda peer: g2s.at[peer], g1.at[d], 0)
    start_all(first, nd)

    def conv_back(x, carry):
        for k in range(2):
            g = 2 * x + k
            start = pl.multiple_of(x * WIN, C)
            conv = mm(gwide[...], gcols[pl.ds(start, KC), k * 256 : k * 256 + 256], NN)
            full = mrow * (conv + bh[g].astype(F32))
            for yo in range(YB):
                for h in range(2):
                    y = 8 * h + YB * k + yo
                    gf[x, pl.ds(y, C, stride=16), :] = full[
                        yo * C : yo * C + C, h * 128 : h * 128 + 128
                    ]
        return carry

    wait_all(first, nd)
    part = g1[0]
    for j in range(1, 8):
        part = part + g1[j]
    g2[b] = part.astype(BF16)
    second = beam_copy(lambda peer, off: g2.at[b], g2.at[b], 5)
    start_all(second, nb)
    for copy in back_halos:
        copy.wait()
    place_halos(gcols, gx, gy, gcn)
    lax.fori_loop(0, 3, conv_back, 0)
    wait_all(second, nb)
    part = g2[0].astype(F32)
    for j in range(1, 16):
        part = part + g2[j].astype(F32)
    g3[d] = part
    third = drift_copy(lambda peer: g3.at[d], g3.at[d], 1)
    start_all(third, nd)
    lax.fori_loop(3, 8, conv_back, 0)
    wait_all(third, nd)
    for j in range(8):
        at = (j // 2) * 216
        gc[(j % 2) * 16 : (j % 2) * 16 + 16, at : at + 216] = g3[j, :, 0:216]


def store(fo, gf, gc, fo_out, gf_out, gc_out, sem):
    copies = [
        pltpu.make_async_copy(src, dst, sem.at[i])
        for i, (src, dst) in enumerate(((gf, gf_out), (fo, fo_out), (gc, gc_out)))
    ]
    for copy in copies:
        copy.start()
    for copy in copies:
        copy.wait()


def body(nd, nb, features, occupied, fragments, cw, emb, mw, uw, es, et, cot):
    vmem = pl.BlockSpec(memory_space=pltpu.VMEM)
    hbm = pl.BlockSpec(memory_space=pltpu.HBM)
    inputs = (
        features.reshape(8, 512, 128),
        occupied.reshape(2, 16),
        fragments,
        cw,
        emb,
        mw,
        uw,
        es.reshape(1, -1),
        et.reshape(1, -1),
        cot,
    )
    scratch = [pltpu.VMEM(one.shape, one.dtype) for one in inputs] + [
        pltpu.SemaphoreType.DMA((10,)),
        pltpu.VMEM((512, 128), F32),
        pltpu.VMEM((C, 27 * C), F32),
        pltpu.VMEM((2, 8, 512, 128), BF16),
        pltpu.VMEM((10 * WIN, 512), BF16),
        pltpu.VMEM((10 * WIN, 512), BF16),
        pltpu.VMEM((YB * C, KC), BF16),
        pltpu.VMEM((YB * C, KC), BF16),
        pltpu.VMEM((16, 256, 1024), BF16),
        pltpu.VMEM((16, 1024, 256), BF16),
        pltpu.VMEM((16, YB * C, 256), BF16),
        pltpu.VMEM((528, 1024), BF16),
        pltpu.VMEM((528, 1024), BF16),
        pltpu.VMEM((16, YB * C, 256), F32),
        pltpu.VMEM((16, YB * C, 256), BF16),
        pltpu.VMEM((2 * YB * C, 512), BF16),
        pltpu.VMEM((2 * YB * C, 512), BF16),
        pltpu.VMEM((528, 256), F32),
        pltpu.VMEM((4 * WIN, 256), F32),
        pltpu.VMEM((2, 512, 128), BF16),
        pltpu.VMEM((2, 8, C, 128), BF16),
        pltpu.VMEM((4, C, 128), BF16),
        pltpu.VMEM((2, 512, 128), BF16),
        pltpu.VMEM((2, 8, C, 128), BF16),
        pltpu.VMEM((4, C, 128), BF16),
        pltpu.VMEM((nb, 8, 256), F32),
        pltpu.VMEM((nb, 8, 256), F32),
        pltpu.VMEM((nb, C, 256), BF16),
        pltpu.VMEM((nb, C, 256), BF16),
        pltpu.VMEM((nb, C, 256), BF16),
        pltpu.VMEM((nb, C, 256), BF16),
        pltpu.VMEM((nb, C, 256), BF16),
        pltpu.VMEM((nb, C, 256), BF16),
        pltpu.VMEM((27 * C, 128), F32),
        pltpu.VMEM((nd, 16, 256), F32),
        pltpu.VMEM((nd, 16, 256), F32),
        pltpu.VMEM((nb, 16, 256), BF16),
        pltpu.VMEM((nd, 16, 256), F32),
        pltpu.SemaphoreType.DMA((16,)),
        pltpu.SemaphoreType.DMA((16,)),
        pltpu.SemaphoreType.DMA((6, nb)),
        pltpu.SemaphoreType.DMA((6, nb)),
        pltpu.SemaphoreType.DMA((2, nd)),
        pltpu.SemaphoreType.DMA((2, nd)),
    ]
    results = pl.pallas_call(
        functools.partial(kernel, nd, nb),
        out_shape=(
            pltpu.VMEM((256, 256), BF16),
            pltpu.VMEM((8, 512, 128), F32),
            pltpu.VMEM((C, 27 * C), F32),
        ),
        in_specs=[hbm] * 10,
        out_specs=(vmem, vmem, vmem),
        scratch_shapes=scratch,
        compiler_params=pltpu.CompilerParams(
            collective_id=0, has_side_effects=True, vmem_limit_bytes=57 << 20
        ),
    )(*[pltpu.with_memory_space_constraint(one, pltpu.HBM) for one in inputs])
    fo, gf, gc = pl.pallas_call(
        store,
        out_shape=tuple(jax.ShapeDtypeStruct(one.shape, one.dtype) for one in results),
        in_specs=[vmem] * 3,
        out_specs=(hbm,) * 3,
        scratch_shapes=[pltpu.SemaphoreType.DMA((3,))],
        compiler_params=pltpu.CompilerParams(vmem_limit_bytes=1 << 20),
    )(*results)
    return fo, gf.reshape(8, C, 16, 128), gc


def solution(mesh):
    return jax.shard_map(
        functools.partial(body, mesh.shape["drift"], mesh.shape["beam"]),
        mesh=mesh,
        in_specs=(
            P("drift", None, "beam", None),
            P("drift", "beam", None),
            P("drift", "beam", None),
            P(),
            P(),
            P(),
            P(),
            P(("drift", "beam")),
            P(("drift", "beam")),
            P(("drift", "beam"), None),
        ),
        out_specs=(P(("drift", "beam"), None), P("drift", None, "beam", None), P()),
        check_vma=False,
    )
```

```python
import functools

import jax
import jax.numpy as jnp
from jax import lax
from jax.experimental import pallas as pl
from jax.experimental.pallas import tpu as pltpu
from jax.sharding import PartitionSpec as P

F32 = jnp.float32
BF16 = jnp.bfloat16
MESH = pl.DeviceIdType.MESH
C = 32
YB = 4
WIN = (YB + 2) * 3 * C
KC = 3 * WIN
NEAR = 9
CLOSE = 6
EC = 1
NN = (((1,), (0,)), ((), ()))
NT = (((1,), (1,)), ((), ()))
TN = (((0,), (0,)), ((), ()))


def mm(lhs, rhs, dims):
    return lax.dot_general(lhs, rhs, dims, preferred_element_type=F32)


def sig_parts(value):
    sig = 0.5 + 0.5 * jnp.tanh(0.5 * value)
    return value * sig, sig * (1.0 + value * (1.0 - sig))


def spread(cols, x, row, tile, lane):
    left = jnp.where(lane == 0, 0.0, pltpu.roll(tile, 1, 1)).astype(BF16)
    right = jnp.where(lane == 127, 0.0, pltpu.roll(tile, 127, 1)).astype(BF16)
    mid = tile.astype(BF16)
    for half in range(2):
        for k in range(2):
            inner = row - 8 * half - 4 * k
            if 0 <= inner < YB + 2:
                for tap, part in enumerate((left, mid, right)):
                    start = pl.multiple_of(x * WIN + inner * 96 + tap * C, C)
                    at = k * 256 + half * 128
                    cols[pl.ds(start, C), at : at + 128] = part


def widen(wide, weight):
    wide[...] = jnp.zeros_like(wide)
    for yo in range(YB):
        for a in range(3):
            at = a * WIN + yo * 96
            wide[yo * C : yo * C + C, at : at + 288] = weight[:, a * 288 : a * 288 + 288].astype(BF16)


def kernel(
    nd,
    nb,
    feat_in,
    occ_in,
    vf_in,
    cw_in,
    emb_in,
    mw_in,
    uw_in,
    es_in,
    et_in,
    cot_in,
    fo,
    gf,
    gc,
    feat,
    occ,
    vf,
    cw,
    emb,
    mw,
    uw,
    es,
    et,
    cot,
    in_sem,
    stage,
    flip,
    plain,
    cols,
    gcols,
    wide,
    gwide,
    lohot,
    lotall,
    hids,
    ahot,
    ahot1,
    slopes,
    bh,
    bc,
    bc1,
    sums,
    gbig,
    hx,
    hy,
    hc,
    gx,
    gy,
    gcn,
    cs,
    cr,
    ms,
    mr,
    pa,
    ms2,
    mr2,
    bm,
    gs,
    g1,
    g2s,
    g2,
    g3,
    hs,
    hr,
    ks,
    kr,
    ps,
    pr,
):
    d = lax.axis_index("drift")
    b = lax.axis_index("beam")
    dn, dp = lax.rem(d + 1, nd), lax.rem(d + nd - 1, nd)
    bn, bp = lax.rem(b + 1, nb), lax.rem(b + nb - 1, nb)

    loads = [
        pltpu.make_async_copy(src, dst, in_sem.at[i])
        for i, (src, dst) in enumerate(
            (
                (occ_in, occ),
                (feat_in, feat),
                (cw_in, cw),
                (vf_in, vf),
                (emb_in, emb),
                (mw_in, mw),
                (uw_in, uw),
                (es_in, es),
                (et_in, et),
                (cot_in, cot),
            )
        )
    ]
    barrier = pltpu.get_barrier_semaphore()

    def greet(dev):
        pl.semaphore_signal(barrier, inc=1, device_id=dev, device_id_type=MESH)

    def greet_beam(off, carry):
        greet((d, lax.rem(b + off, nb)))
        return carry

    def greet_drift(off, carry):
        greet((lax.rem(d + off, nd), b))
        return carry

    lax.fori_loop(1, nb, greet_beam, 0)
    lax.fori_loop(1, nd, greet_drift, 0)
    for dev in ((dn, bn), (dn, bp), (dp, bn), (dp, bp)):
        greet(dev)
    for copy in loads:
        copy.start()
    loads[0].wait()
    loads[1].wait()

    lane = lax.broadcasted_iota(jnp.int32, (C, 128), 1)
    square = (C, C)
    eye = (
        lax.broadcasted_iota(jnp.int32, square, 0) == lax.broadcasted_iota(jnp.int32, square, 1)
    ).astype(F32).astype(BF16)
    group = lax.broadcasted_iota(jnp.int32, (1, 128), 1) // 8
    occ_f = occ[...].astype(F32)
    rows = []
    for j in range(2):
        row = jnp.zeros((1, 128), F32)
        for q in range(16):
            row = jnp.where(group == q, occ_f[j : j + 1, q : q + 1], row)
        rows.append(row)
    mrow = jnp.concatenate(rows, axis=1)
    x_lo = jnp.where(d > 0, 1.0, 0.0).astype(F32)
    x_hi = jnp.where(d < nd - 1, 1.0, 0.0).astype(F32)
    y_lo = jnp.where(b > 0, 1.0, 0.0).astype(F32)
    y_hi = jnp.where(b < nb - 1, 1.0, 0.0).astype(F32)

    def halo_copies(src, tx, ty, tc, base):
        plan = (
            (src.at[7, 480:512, :], tc.at[0], (dn, bn)),
            (src.at[7, 0:32, :], tc.at[1], (dn, bp)),
            (src.at[0, 480:512, :], tc.at[2], (dp, bn)),
            (src.at[0, 0:32, :], tc.at[3], (dp, bp)),
            (src.at[:, 480:512, :], ty.at[0], (d, bn)),
            (src.at[:, 0:32, :], ty.at[1], (d, bp)),
            (src.at[7], tx.at[0], (dn, b)),
            (src.at[0], tx.at[1], (dp, b)),
        )
        return [
            pltpu.make_async_remote_copy(
                src_ref=s,
                dst_ref=t,
                send_sem=hs.at[base + i],
                recv_sem=hr.at[base + i],
                device_id=dev,
                device_id_type=MESH,
            )
            for i, (s, t, dev) in enumerate(plan)
        ]

    def place_halos(target, tx, ty, tc):
        for y in range(16):
            spread(target, 0, y + 1, tx[0, y * C : y * C + C, :].astype(F32) * x_lo, lane)
            spread(target, 9, y + 1, tx[1, y * C : y * C + C, :].astype(F32) * x_hi, lane)

        def per_x(x, carry):
            spread(target, x + 1, 0, ty[0, x].astype(F32) * y_lo, lane)
            spread(target, x + 1, 17, ty[1, x].astype(F32) * y_hi, lane)
            return carry

        lax.fori_loop(0, 8, per_x, 0)
        spread(target, 0, 0, tc[0].astype(F32) * (x_lo * y_lo), lane)
        spread(target, 0, 17, tc[1].astype(F32) * (x_lo * y_hi), lane)
        spread(target, 9, 0, tc[2].astype(F32) * (x_hi * y_lo), lane)
        spread(target, 9, 17, tc[3].astype(F32) * (x_hi * y_hi), lane)

    by, bz = lax.rem(b, 4), b // 4
    near = sorted(range(16), key=lambda o: min(o % 4, 4 - o % 4) + min(o // 4, 4 - o // 4))
    far = near[:0:-1]

    def beam_copy(src, dst, base):
        def make(off):
            peer = 4 * lax.rem(bz + off // 4, 4) + lax.rem(by + off % 4, 4)
            return pltpu.make_async_remote_copy(
                src_ref=src(peer, off),
                dst_ref=dst(off) if callable(dst) else dst,
                send_sem=ks.at[base, off],
                recv_sem=kr.at[base, off],
                device_id=(d, peer),
                device_id_type=MESH,
            )

        return make

    def drift_copy(src, dst, base):
        def make(off):
            peer = lax.rem(d + off, nd)
            return pltpu.make_async_remote_copy(
                src_ref=src(peer),
                dst_ref=dst,
                send_sem=ps.at[base, off],
                recv_sem=pr.at[base, off],
                device_id=(peer, b),
                device_id_type=MESH,
            )

        return make

    def start_all(make, count):
        for off in far if count == nb else range(1, count):
            make(off).start()

    def wait_all(make, count):
        for off in range(1, count):
            make(off).wait()

    def load_row(x, carry):
        stage[...] = feat[x].astype(F32)
        for y in range(16):
            h = y // 8
            tile = stage[pl.ds(y, C, stride=16), :] * mrow[:, h * 128 : h * 128 + 128]
            plain[0, x, y * C : y * C + C, :] = tile.astype(BF16)
            spread(cols, x + 1, y + 1, tile, lane)
        return carry

    lax.fori_loop(0, 8, load_row, 0)
    pl.semaphore_wait(barrier, nb - 1 + nd - 1 + 4)
    halos = halo_copies(plain.at[0], hx, hy, hc, 0)
    for copy in halos:
        copy.start()

    sub_hi = lax.broadcasted_iota(jnp.int32, (16, 256), 0)
    sub_b = sub_hi.astype(F32).astype(BF16)
    one_b = jnp.ones((16, 256), BF16)
    zero_b = jnp.zeros((16, 256), BF16)
    lane_b = lax.broadcasted_iota(jnp.int32, (256, 128), 1).astype(F32).astype(BF16)
    one_c = jnp.ones((256, 128), BF16)
    zero_c = jnp.zeros((256, 128), BF16)

    def fids(x):
        return jnp.concatenate([vf[x, 0:8, :], vf[x, 8:16, :]], axis=1)

    def shift_of(x, sign):
        hi = fids(x) >> 8
        return ((((hi >> 2) - bz) * sign & 3) << 2) + (((hi & 3) - by) * sign & 3)

    def one_hots(x, carry):
        ids = fids(x) & 255
        columns = ids.astype(F32).T
        for k in range(2):
            for yo in range(YB):
                r = k * YB + yo
                col = jnp.broadcast_to(columns[:, r : r + 1], (256, 128)).astype(BF16)
                for j in range(2):
                    lotall[2 * x + k, yo * 256 : yo * 256 + 256, j * 128 : j * 128 + 128] = jnp.where(
                        col == lane_b + BF16(128 * j), one_c, zero_c
                    )
                lo_b = jnp.broadcast_to(ids[r : r + 1, :], (16, 256)).astype(F32).astype(BF16)
                for j in range(16):
                    lohot[2 * x + k, j * 16 : j * 16 + 16, yo * 256 : yo * 256 + 256] = jnp.where(
                        sub_b == lo_b - BF16(16 * j), one_b, zero_b
                    )
        return carry

    loads[3].wait()
    lax.fori_loop(0, 8, one_hots, 0)

    loads[2].wait()
    widen(wide, cw)
    turned = mm(cw[...], eye, TN)
    for t in range(27):
        flip[:, (26 - t) * C : (27 - t) * C] = turned[t * C : t * C + C, :]
    widen(gwide, flip)
    for copy in halos:
        copy.wait()
    place_halos(cols, hx, hy, hc)

    sums[...] = jnp.zeros_like(sums)

    zero_h = jnp.zeros((C, 256), BF16)

    def fill(hot, r, shifts, hid, first, last):
        yo = r % YB
        row = jnp.broadcast_to(shifts[r : r + 1, :], (C, 256)).astype(F32).astype(BF16)
        for p in range(first, last):
            hot[p * C : p * C + C, yo * 256 : yo * 256 + 256] = jnp.where(
                row == BF16(near[p]), hid, zero_h
            )

    def convolve(x, k, hot):
        shifts = shift_of(x, 1)
        owners = fids(x) >> 8
        start = pl.multiple_of(x * WIN, C)
        conv = mm(wide[...], cols[pl.ds(start, KC), k * 256 : k * 256 + 256], NN)
        slopes[2 * x + k] = conv
        half = 0.5 * conv
        silu = half + half * jnp.tanh(half)
        for yo in range(YB):
            at = pl.multiple_of((x + 1) * WIN + (yo + 1) * 96 + C, C)
            act = cols[pl.ds(at, C), k * 256 : k * 256 + 256].astype(F32)
            hid = (mrow * (act + silu[yo * C : yo * C + C, :])).astype(BF16)
            hids[2 * x + k, yo * C : yo * C + C, :] = hid
            r = k * YB + yo
            fill(hot, r, shifts, hid, NEAR, 16)
            hot[512:528, yo * 256 : yo * 256 + 256] = jnp.where(
                sub_hi == owners[r : r + 1, :], mrow, 0.0
            ).astype(BF16)

    def refill(x, k, hot):
        shifts = shift_of(x, 1)
        for yo in range(YB):
            fill(hot, k * YB + yo, shifts, hids[2 * x + k, yo * C : yo * C + C, :], 0, NEAR)

    def scatter_far(g, hot):
        sums[NEAR * C : 528, :] += mm(hot[NEAR * C : 528, :], lotall[g], NN)

    def scatter_near(g, hot):
        sums[0 : NEAR * C, :] += mm(hot[0 : NEAR * C, :], lotall[g], NN)

    def two_stage(make, use):
        def step(x, carry):
            use(2 * x, ahot)
            make(x, 1, ahot1)
            use(2 * x + 1, ahot1)
            make(x + 1, 0, ahot)
            return carry

        make(0, 0, ahot)
        lax.fori_loop(0, 7, step, 0)
        use(14, ahot)
        make(7, 1, ahot1)
        use(15, ahot1)

    sum_copies = beam_copy(
        lambda peer, off: ms.at[near.index(off)], lambda off: mr.at[near.index(off)], 1
    )
    two_stage(convolve, scatter_far)
    for p in range(15, NEAR - 1, -1):
        ms[p] = sums[p * C : p * C + C, :].astype(BF16)
        sum_copies(near[p]).start()
    for j in range(16):
        cs[j] = jnp.broadcast_to(sums[512 + j : 513 + j, :], (8, 256))
    cr[b] = cs[b]
    count_copies = beam_copy(lambda peer, off: cs.at[peer], cr.at[b], 0)
    start_all(count_copies, nb)
    two_stage(refill, scatter_near)
    for p in range(NEAR - 1, 0, -1):
        ms[p] = sums[p * C : p * C + C, :].astype(BF16)
        sum_copies(near[p]).start()
    mr[0] = sums[0:C, :].astype(BF16)

    def slope_of(g, carry):
        sig = 0.5 + 0.5 * jnp.tanh(0.5 * slopes[g])
        slopes[g] = mrow * (sig * (1.0 + slopes[g] * (1.0 - sig)))
        return carry

    lax.fori_loop(0, 16, slope_of, 0)

    for i in range(4, 10):
        loads[i].wait()
    sub_e = lax.broadcasted_iota(jnp.int32, (256, 1024), 0)
    src = es[...]
    src_lo = (sub_e == (src & 255)).astype(F32).astype(BF16)
    src_hi = src >> 8
    dst_hot = (sub_e == et[...]).astype(F32).astype(BF16)
    back_agg = mm(cot[...], uw[...], NT).astype(BF16)
    agg_edge = mm(back_agg, dst_hot, TN)

    wait_all(count_copies, nb)
    wait_all(sum_copies, nb)
    total = mr[0].astype(F32)
    number = cr[0]
    for j in range(1, 16):
        total = total + mr[j].astype(F32)
        number = number + cr[j]
    inverse = 1.0 / jnp.maximum(number[0:1, :], 1.0)
    pooled = (total * inverse).astype(BF16)
    pa[b] = pooled
    pool_copies = beam_copy(lambda peer, off: pa.at[b], pa.at[b], 2)
    start_all(pool_copies, nb)

    pre_own = mm(pooled, emb[...], TN)
    silu_own, slope_own = sig_parts(pre_own)
    own = silu_own.astype(BF16)
    back_self = mm(emb[...], (cot[...].astype(F32) * slope_own).astype(BF16), NT)

    wait_all(pool_copies, nb)
    table = pa[...].reshape(16 * C, 256)
    msgs = []
    for e in range(EC):
        w = 1024 // EC
        cut = slice(e * w, e * w + w)
        every = mm(table, src_lo[:, cut], NN)
        picked = every[0:C, :]
        for q in range(1, 16):
            picked = jnp.where(src_hi[:, cut] == q, every[q * C : q * C + C, :], picked)
        pre_src = mm(emb[...], picked.astype(BF16), TN)
        silu_src, slope_src = sig_parts(pre_src)
        pre_msg = mm(mw[...], silu_src.astype(BF16), TN)
        silu_msg, slope_msg = sig_parts(pre_msg)
        msgs.append(silu_msg.astype(BF16))
        back_pre = (agg_edge[:, cut] * slope_msg).astype(BF16)
        back_src = mm(mw[...], back_pre, NN)
        back_edge = mm(emb[...], (back_src * slope_src).astype(BF16), NN)
        for q in range(16):
            ahot[q * C : q * C + C, cut] = jnp.where(src_hi[:, cut] == q, back_edge, 0.0).astype(
                BF16
            )
    back_sums = mm(ahot[0:512, :], src_lo, NT)
    for j in range(16):
        ms2[j] = back_sums[j * C : j * C + C, :].astype(BF16)
    mr2[b] = ms2[b]
    back_copies = beam_copy(lambda peer, off: ms2.at[peer], mr2.at[b], 1)
    start_all(back_copies, nb)

    gathered = mm(dst_hot, jnp.concatenate(msgs, axis=1), NT).astype(BF16)
    fo[...] = (own.astype(F32) + mm(gathered, uw[...], NN)).astype(BF16)

    wait_all(back_copies, nb)
    remote = back_self
    for j in range(16):
        remote = remote + mr2[j].astype(F32)
    bm[0] = (remote * inverse).astype(BF16)
    mean_copies = beam_copy(lambda peer, off: bm.at[0], lambda off: bm.at[near.index(off)], 2)
    for off in near[1:]:
        mean_copies(off).start()
    gbig[...] = jnp.zeros_like(gbig)
    for off in near[1:CLOSE]:
        mean_copies(off).wait()

    def gather_near(x, carry):
        shifts = shift_of(x, -1)
        means = bm[0:CLOSE].reshape(CLOSE * C, 256)
        for k in range(2):
            for yo in range(YB):
                r = k * YB + yo
                hi = shifts[r : r + 1, :]
                got = mm(means, lohot[2 * x + k, :, yo * 256 : yo * 256 + 256], NN)
                hid = got[0:C, :]
                for q in range(1, CLOSE):
                    hid = jnp.where(hi == near[q], got[q * C : q * C + C, :], hid)
                bh[2 * x + k, yo * C : yo * C + C, :] = hid.astype(BF16)
        return carry

    lax.fori_loop(0, 8, gather_near, 0)
    for off in near[CLOSE:]:
        mean_copies(off).wait()

    def gather_far(i, out):
        means = bm[CLOSE:16].reshape((16 - CLOSE) * C, 256)
        for j in range(2):
            x = 2 * i + j
            shifts = shift_of(x, -1)
            for k in range(2):
                g = 2 * x + k
                for yo in range(YB):
                    r = k * YB + yo
                    hi = shifts[r : r + 1, :]
                    got = mm(means, lohot[g, :, yo * 256 : yo * 256 + 256], NN)
                    hid = bh[g, yo * C : yo * C + C, :].astype(F32)
                    for q in range(CLOSE, 16):
                        at = (q - CLOSE) * C
                        hid = jnp.where(hi == near[q], got[at : at + C, :], hid)
                    bh[g, yo * C : yo * C + C, :] = hid.astype(BF16)
                    back = hid * slopes[g, yo * C : yo * C + C, :]
                    row = j * YB * C + yo * C
                    out[row : row + C, k * 256 : k * 256 + 256] = back.astype(BF16)
                    for h in range(2):
                        y = 8 * h + YB * k + yo
                        tile = back[:, h * 128 : h * 128 + 128]
                        plain[1, x, y * C : y * C + C, :] = tile.astype(BF16)
                        spread(gcols, x + 1, y + 1, tile, lane)

    def weights(i, back):
        start = pl.multiple_of(2 * i * WIN, C)
        gbig[...] += mm(cols[pl.ds(start, 4 * WIN), :], back[...], NT)

    def backward(i, carry):
        weights(i, bc)
        gather_far(i + 1, bc1)
        bc[...] = bc1[...]
        return carry

    gather_far(0, bc)
    lax.fori_loop(0, 3, backward, 0)
    back_halos = halo_copies(plain.at[1], gx, gy, gcn, 8)
    for copy in back_halos:
        copy.start()
    weights(3, bc)
    quarter = lax.broadcasted_iota(jnp.int32, (288, 128), 1) // C
    for a in range(3):
        total = None
        for j in range(2):
            at = (j + a) * WIN
            part = gbig[at : at + 288, j * 128 : j * 128 + 128]
            for yo in range(1, YB):
                down = at + yo * 96
                part = jnp.where(
                    quarter == yo, gbig[down : down + 288, j * 128 : j * 128 + 128], part
                )
            total = part if total is None else total + part
        total = total + pltpu.roll(total, 64, 1)
        gs[a * 288 : a * 288 + 288, :] = total + pltpu.roll(total, 32, 1)
    packed = gs[0:216, :]
    for j in range(1, 4):
        packed = jnp.where(quarter[0:216] == j, gs[j * 216 : j * 216 + 216, :], packed)
    turned = jnp.concatenate([packed, jnp.zeros((40, 128), F32)], axis=0).T
    for j in range(8):
        g2s[j] = turned[j * 16 : j * 16 + 16, :]
    g1[d] = g2s[d]
    first = drift_copy(lambda peer: g2s.at[peer], g1.at[d], 0)
    start_all(first, nd)

    def conv_back(x, carry):
        for k in range(2):
            g = 2 * x + k
            start = pl.multiple_of(x * WIN, C)
            conv = mm(gwide[...], gcols[pl.ds(start, KC), k * 256 : k * 256 + 256], NN)
            full = mrow * (conv + bh[g].astype(F32))
            for yo in range(YB):
                for h in range(2):
                    y = 8 * h + YB * k + yo
                    gf[x, pl.ds(y, C, stride=16), :] = full[
                        yo * C : yo * C + C, h * 128 : h * 128 + 128
                    ]
        return carry

    wait_all(first, nd)
    part = g1[0]
    for j in range(1, 8):
        part = part + g1[j]
    g2[b] = part.astype(BF16)
    second = beam_copy(lambda peer, off: g2.at[b], g2.at[b], 1)
    start_all(second, nb)
    for copy in back_halos:
        copy.wait()
    place_halos(gcols, gx, gy, gcn)
    lax.fori_loop(0, 3, conv_back, 0)
    wait_all(second, nb)
    part = g2[0].astype(F32)
    for j in range(1, 16):
        part = part + g2[j].astype(F32)
    g3[d] = part
    third = drift_copy(lambda peer: g3.at[d], g3.at[d], 1)
    start_all(third, nd)
    lax.fori_loop(3, 8, conv_back, 0)
    wait_all(third, nd)
    for j in range(8):
        at = (j // 2) * 216
        gc[(j % 2) * 16 : (j % 2) * 16 + 16, at : at + 216] = g3[j, :, 0:216]


def store(fo, gf, gc, fo_out, gf_out, gc_out, sem):
    copies = [
        pltpu.make_async_copy(src, dst, sem.at[i])
        for i, (src, dst) in enumerate(((gf, gf_out), (fo, fo_out), (gc, gc_out)))
    ]
    for copy in copies:
        copy.start()
    for copy in copies:
        copy.wait()


def body(nd, nb, features, occupied, fragments, cw, emb, mw, uw, es, et, cot):
    vmem = pl.BlockSpec(memory_space=pltpu.VMEM)
    hbm = pl.BlockSpec(memory_space=pltpu.HBM)
    inputs = (
        features.reshape(8, 512, 128),
        occupied.reshape(2, 16),
        fragments,
        cw,
        emb,
        mw,
        uw,
        es.reshape(1, -1),
        et.reshape(1, -1),
        cot,
    )
    scratch = [pltpu.VMEM(one.shape, one.dtype) for one in inputs] + [
        pltpu.SemaphoreType.DMA((10,)),
        pltpu.VMEM((512, 128), F32),
        pltpu.VMEM((C, 27 * C), F32),
        pltpu.VMEM((2, 8, 512, 128), BF16),
        pltpu.VMEM((10 * WIN, 512), BF16),
        pltpu.VMEM((10 * WIN, 512), BF16),
        pltpu.VMEM((YB * C, KC), BF16),
        pltpu.VMEM((YB * C, KC), BF16),
        pltpu.VMEM((16, 256, 1024), BF16),
        pltpu.VMEM((16, 1024, 256), BF16),
        pltpu.VMEM((16, YB * C, 256), BF16),
        pltpu.VMEM((528, 1024), BF16),
        pltpu.VMEM((528, 1024), BF16),
        pltpu.VMEM((16, YB * C, 256), F32),
        pltpu.VMEM((16, YB * C, 256), BF16),
        pltpu.VMEM((2 * YB * C, 512), BF16),
        pltpu.VMEM((2 * YB * C, 512), BF16),
        pltpu.VMEM((528, 256), F32),
        pltpu.VMEM((4 * WIN, 256), F32),
        pltpu.VMEM((2, 512, 128), BF16),
        pltpu.VMEM((2, 8, C, 128), BF16),
        pltpu.VMEM((4, C, 128), BF16),
        pltpu.VMEM((2, 512, 128), BF16),
        pltpu.VMEM((2, 8, C, 128), BF16),
        pltpu.VMEM((4, C, 128), BF16),
        pltpu.VMEM((nb, 8, 256), F32),
        pltpu.VMEM((nb, 8, 256), F32),
        pltpu.VMEM((nb, C, 256), BF16),
        pltpu.VMEM((nb, C, 256), BF16),
        pltpu.VMEM((nb, C, 256), BF16),
        pltpu.VMEM((nb, C, 256), BF16),
        pltpu.VMEM((nb, C, 256), BF16),
        pltpu.VMEM((nb, C, 256), BF16),
        pltpu.VMEM((27 * C, 128), F32),
        pltpu.VMEM((nd, 16, 256), F32),
        pltpu.VMEM((nd, 16, 256), F32),
        pltpu.VMEM((nb, 16, 256), BF16),
        pltpu.VMEM((nd, 16, 256), F32),
        pltpu.SemaphoreType.DMA((16,)),
        pltpu.SemaphoreType.DMA((16,)),
        pltpu.SemaphoreType.DMA((3, nb)),
        pltpu.SemaphoreType.DMA((3, nb)),
        pltpu.SemaphoreType.DMA((2, nd)),
        pltpu.SemaphoreType.DMA((2, nd)),
    ]
    results = pl.pallas_call(
        functools.partial(kernel, nd, nb),
        out_shape=(
            pltpu.VMEM((256, 256), BF16),
            pltpu.VMEM((8, 512, 128), F32),
            pltpu.VMEM((C, 27 * C), F32),
        ),
        in_specs=[hbm] * 10,
        out_specs=(vmem, vmem, vmem),
        scratch_shapes=scratch,
        compiler_params=pltpu.CompilerParams(
            collective_id=0, has_side_effects=True, vmem_limit_bytes=57 << 20
        ),
    )(*[pltpu.with_memory_space_constraint(one, pltpu.HBM) for one in inputs])
    fo, gf, gc = pl.pallas_call(
        store,
        out_shape=tuple(jax.ShapeDtypeStruct(one.shape, one.dtype) for one in results),
        in_specs=[vmem] * 3,
        out_specs=(hbm,) * 3,
        scratch_shapes=[pltpu.SemaphoreType.DMA((3,))],
        compiler_params=pltpu.CompilerParams(vmem_limit_bytes=1 << 20),
    )(*results)
    return fo, gf.reshape(8, C, 16, 128), gc


def solution(mesh):
    return jax.shard_map(
        functools.partial(body, mesh.shape["drift"], mesh.shape["beam"]),
        mesh=mesh,
        in_specs=(
            P("drift", None, "beam", None),
            P("drift", "beam", None),
            P("drift", "beam", None),
            P(),
            P(),
            P(),
            P(),
            P(("drift", "beam")),
            P(("drift", "beam")),
            P(("drift", "beam"), None),
        ),
        out_specs=(P(("drift", "beam"), None), P("drift", None, "beam", None), P()),
        check_vma=False,
    )
```
